128 devices in a mesh: pipe: 32 (over y, z, x_hi), expert: 4 (over x_lo, core).
Axes of the slice: x: 4 (x_hi: 2, x_lo: 2; x = x_hi * 2 + x_lo), y: 4, z: 4, core: 2. Of those that a mesh axis runs over, the one named last changes fastest.
Arguments:
- fwd_in: bfloat16 [16384, 3584], P(('pipe', 'expert')), may hold values from -6 to 6
- fwd_routes: int32 [16384, 2], P(('pipe', 'expert')), may hold values from 0 to 3, all different within a row; in each aligned block of 128 rows (0 to 127, 128 to 255, ...) at most 96 rows name the same one
- saved_in: bfloat16 [16384, 3584], P(('pipe', 'expert')), may hold values from -6 to 6
- saved_routes: int32 [16384, 2], P(('pipe', 'expert')), may hold values from 0 to 3, all different within a row; in each aligned block of 128 rows (0 to 127, 128 to 255, ...) at most 96 rows name the same one
- grad_in: bfloat16 [16384, 3584], P(('pipe', 'expert')), may hold values from -6 to 6
- norm_gain: float32 [32, 3584], P('pipe'), may hold values from 0.25 to 1.75
- router: bfloat16 [32, 3584, 4], P('pipe'), may hold values from -0.09375 to 0.09375
- w_gate: bfloat16 [32, 4, 3584, 1024], P('pipe', 'expert'), may hold values from -0.09375 to 0.09375
- w_up: bfloat16 [32, 4, 3584, 1024], P('pipe', 'expert'), may hold values from -0.09375 to 0.09375
- w_down: bfloat16 [32, 4, 1024, 3584], P('pipe', 'expert'), may hold values from -0.1875 to 0.1875
Outputs:
- fwd_out: bfloat16 [16384, 3584], P(('pipe', 'expert'))
- grad_out: bfloat16 [16384, 3584], P(('pipe', 'expert'))
The draws below stay inside these ranges and needn't reach their ends.
Inputs may be any that keep to these rules, and one draw needn't show every extreme that they name: `fwd_routes`: each row names 2 different experts; among the rows of one device no expert is named by more than 96 rows, a bound that some block reaches. `saved_routes`: each row names 2 different experts; among the rows of one device no expert is named by more than 96 rows, a bound that some block reaches.
All inputs are finite; a program needn't handle non-finite values.
Results may differ from the reference program's by a relative error of at most 0.0057.
Values may be sent and summed in bfloat16 or wider, within the bound.
A program may use at most 128 MiB of HBM per device.

```python
import math
import jax
import jax.numpy as jnp
import numpy as np
from jax import lax

D = 3584
F = 1024
TOP = 2
TOK_DEV = 128
EXPERTS = 4
CAP = 96
TOKENS = 16384
N_PIPE = 32
N_EXPERT = 4


def steps_of(key, shape, shards, smallest, largest):
    gain, own = 1.0, jax.random.fold_in(key, 6)
    for dim, blocks in shards:
        draws = jnp.exp(jax.random.uniform(jax.random.fold_in(own, dim), (blocks,), jnp.float32, smallest / len(shards), largest / len(shards)))
        gain = gain * jnp.repeat(draws, shape[dim] // blocks).reshape([-1 if axis == dim else 1 for axis in range(len(shape))])
    return gain


def routed_block(stream_key, own, number, rows, number_of, top, bound, skew):
    sequence = jax.random.permutation(stream_key, number_of)
    crowded, common = portions_of(number_of, rows * top, bound, skew, True), portions_of(number_of, rows * top, bound, skew, False)
    places = jnp.arange(number_of)

    def named(lengths, turn):
        used = int((lengths > 0).sum())
        fixed = max(1, used // 4)
        passed = fixed + (places - fixed + turn * (used - fixed)) % max(1, number_of - fixed)
        return jnp.zeros((number_of,), jnp.int32).at[sequence[jnp.where(places < fixed, places, passed)]].set(jnp.asarray(lengths, jnp.int32))

    lengths = jnp.where(number % 4 == 0, named(crowded, number // 4), named(common, number - number // 4 - 1))
    mixed = jax.random.permutation(jax.random.fold_in(own, 3), number_of)
    donor, sink = mixed[0:number_of // 2 * 2:2], mixed[1:number_of // 2 * 2:2]
    slack = jnp.minimum(lengths[donor] - 1, bound - lengths[sink]) // 2
    slack = jnp.where((donor == sequence[0]) | (sink == sequence[0]) | (lengths[sink] == 0), 0, jnp.maximum(slack, 0))
    passed = jax.random.randint(jax.random.fold_in(own, 4), (number_of // 2,), 0, 1 << 20) % (slack + 1)
    lengths = lengths.at[donor].add(-passed).at[sink].add(passed)
    members = jnp.searchsorted(jnp.cumsum(lengths), jnp.arange(rows * top), side="right").astype(jnp.int32)
    grid = members.reshape(top, rows).T
    grid = grid[jax.random.permutation(jax.random.fold_in(own, 1), rows)]
    turn = jax.random.randint(jax.random.fold_in(own, 2), (rows, 1), 0, top)
    return jnp.take_along_axis(grid, (jnp.arange(top)[None, :] + turn) % top, axis=1)


def portions_of(count, total, most, skew, full):
    loads = [(1 << 20) // math.isqrt(rank ** skew) + 1 for rank in range(1, count + 1)]
    largest = most if full else min(most, max(-(-total // count), total * loads[0] // sum(loads)))
    least = 1 if total - largest >= count - 1 else 0
    counts, surplus = [largest] + [least] * (count - 1), total - largest - least * (count - 1)
    while surplus > 0:
        movable = [i for i in range(1, count) if counts[i] < largest] or [i for i in range(1, count) if counts[i] < most]
        whole, remaining = sum([loads[i] for i in movable]), surplus
        for i in movable:
            more = min(most - counts[i], max(1, remaining * loads[i] // whole), surplus)
            counts[i] = counts[i] + more
            surplus = surplus - more
    return np.array(counts)


def noise(rng, dims, spread, most, shards=(), kind=jnp.bfloat16):
    factor_of = steps_of(rng, dims, shards, -0.22, 0.18) if shards else 1.0
    values = jax.random.normal(rng, dims, jnp.float32) * spread * factor_of
    return jnp.minimum(jnp.maximum(values, -most), most).astype(kind)


def setup_inputs(seed: int = 0) -> dict:
    splits = jax.random.split(jax.random.key(seed), 11)
    fwd_in = noise(splits[0], (TOKENS, D), 1.0, 6.0, ((0, 128),))
    fwd_routes_keys = jax.random.split(jax.random.fold_in(splits[1], 1), TOKENS // TOK_DEV)
    fwd_routes_turns = jax.random.permutation(jax.random.fold_in(splits[1], 3), TOKENS // TOK_DEV)
    fwd_routes = jax.vmap(lambda own, number: routed_block(jax.random.fold_in(splits[1], 2), own, number, TOK_DEV, EXPERTS, TOP, CAP, 1))(fwd_routes_keys, fwd_routes_turns).reshape((TOKENS, TOP))
    saved_in = noise(splits[2], (TOKENS, D), 1.0, 6.0, ((0, 128),))
    saved_routes_keys = jax.random.split(jax.random.fold_in(splits[3], 1), TOKENS // TOK_DEV)
    saved_routes_turns = jax.random.permutation(jax.random.fold_in(splits[3], 3), TOKENS // TOK_DEV)
    saved_routes = jax.vmap(lambda own, number: routed_block(jax.random.fold_in(splits[3], 2), own, number, TOK_DEV, EXPERTS, TOP, CAP, 1))(saved_routes_keys, saved_routes_turns).reshape((TOKENS, TOP))
    grad_in = noise(splits[4], (TOKENS, D), 1.0, 6.0, ((0, 128),))
    norm_gain = jnp.clip(1.0 + 0.15 * jax.random.normal(splits[5], (N_PIPE, D), jnp.float32), 0.25, 1.75)
    router = noise(splits[6], (N_PIPE, D, EXPERTS), D ** -0.5, 0.09375, ((0, 32),))
    w_gate = noise(splits[7], (N_PIPE, EXPERTS, D, F), D ** -0.5, 0.09375, ((0, 32), (1, 4)))
    w_up = noise(splits[8], (N_PIPE, EXPERTS, D, F), D ** -0.5, 0.09375, ((0, 32), (1, 4)))
    w_down = noise(splits[9], (N_PIPE, EXPERTS, F, D), F ** -0.5, 0.1875, ((0, 32), (1, 4)))
    return {"fwd_in": fwd_in, "fwd_routes": fwd_routes, "saved_in": saved_in, "saved_routes": saved_routes, "grad_in": grad_in, "norm_gain": norm_gain, "router": router, "w_gate": w_gate, "w_up": w_up, "w_down": w_down}


EPSILON = 1e-06

def normalize(in_rows, gain_row):
    widened = in_rows.astype(jnp.float32)
    inv_rms = lax.rsqrt(lax.optimization_barrier(jnp.mean(widened * widened, axis=-1, keepdims=True)) + EPSILON)
    normed = (widened * inv_rms * gain_row).astype(jnp.bfloat16)
    return (widened, inv_rms, normed)

def route_weights(normed, router_cols, route_ids):
    logits = jnp.dot(normed, router_cols, preferred_element_type=jnp.float32)
    scores = jax.nn.sigmoid(logits)
    expert_ids = jnp.arange(router_cols.shape[1], dtype=jnp.int32)
    picked = (route_ids[:, :, None] == expert_ids[None, None, :]).astype(jnp.float32)
    chosen = lax.optimization_barrier(jnp.sum(picked * scores[:, None, :], axis=-1))
    summed = lax.optimization_barrier(jnp.sum(chosen, axis=-1, keepdims=True))
    return (picked, chosen, summed, chosen / summed)

def expert_forward(normed, gate_w, up_w, down_w):
    gate_pre = jnp.dot(normed, gate_w, preferred_element_type=jnp.float32)
    up_pre = jnp.dot(normed, up_w, preferred_element_type=jnp.float32)
    hidden = (jax.nn.silu(gate_pre) * up_pre).astype(jnp.bfloat16)
    output = jnp.dot(hidden, down_w, preferred_element_type=jnp.float32).astype(jnp.bfloat16)
    return (gate_pre, up_pre, output)

def expert_backward(normed, grad_rows, gate_w, up_w, down_w):
    gate_pre, up_pre, output = expert_forward(normed, gate_w, up_w, down_w)
    dhidden = jnp.dot(grad_rows, down_w.T, preferred_element_type=jnp.float32)
    sigmoid_gate = jax.nn.sigmoid(gate_pre)
    dgate = (dhidden * up_pre * sigmoid_gate * (1.0 + gate_pre * (1.0 - sigmoid_gate))).astype(jnp.bfloat16)
    dupper = (dhidden * jax.nn.silu(gate_pre)).astype(jnp.bfloat16)
    dnormed = (jnp.dot(dgate, gate_w.T, preferred_element_type=jnp.float32) + jnp.dot(dupper, up_w.T, preferred_element_type=jnp.float32)).astype(jnp.bfloat16)
    dprob = lax.optimization_barrier(jnp.sum(grad_rows.astype(jnp.float32) * output.astype(jnp.float32), axis=-1)).astype(jnp.bfloat16)
    return (dnormed, dprob)

def input_gradient(grad_rows, widened, inv_rms, gain_row, router_cols, picked, chosen, summed, probs, dnorm_all, dprob_all):
    mixed_dot = lax.optimization_barrier(jnp.sum(dprob_all * probs, axis=-1, keepdims=True))
    dchosen = (dprob_all - mixed_dot) / summed
    dlogit_sel = dchosen * chosen * (1.0 - chosen)
    dlogits = lax.optimization_barrier(jnp.sum(picked * dlogit_sel[:, :, None], axis=1))
    dnorm_all = dnorm_all + jnp.dot(dlogits, router_cols.astype(jnp.float32).T, precision=lax.Precision.HIGHEST)
    scaled_grad = dnorm_all * gain_row
    dinput = inv_rms * scaled_grad - widened * inv_rms ** 3 * lax.optimization_barrier(jnp.mean(scaled_grad * widened, axis=-1, keepdims=True))
    return (grad_rows.astype(jnp.float32) + dinput).astype(jnp.bfloat16)

def expert_rows(route_ids, expert, limit):
    is_hit = jnp.any(route_ids == expert, axis=-1)
    picked_rows = jnp.nonzero(is_hit, size=limit, fill_value=0)[0].astype(jnp.int32)
    hit_count = jnp.sum(is_hit.astype(jnp.int32))
    is_valid = (jnp.arange(limit, dtype=jnp.int32) < hit_count).astype(jnp.float32)
    return (picked_rows, is_valid)

def group_forward(in_rows, route_ids, gain_row, router_cols, gate_mats, up_mats, down_mats):
    widened, inv_rms, normed = normalize(in_rows, gain_row)
    picked, chosen, summed, probs = route_weights(normed, router_cols, route_ids)
    result = widened
    limit = N_EXPERT * CAP
    for expert in range(EXPERTS):
        picked_rows, is_valid = expert_rows(route_ids, expert, limit)
        weight = lax.optimization_barrier(jnp.sum(picked[:, :, expert] * probs, axis=-1))[picked_rows] * is_valid
        _, _, output = expert_forward(normed[picked_rows], gate_mats[expert], up_mats[expert], down_mats[expert])
        result = result.at[picked_rows].add(weight[:, None] * output.astype(jnp.float32))
    return result.astype(jnp.bfloat16)

def group_backward(in_rows, route_ids, grad_rows, gain_row, router_cols, gate_mats, up_mats, down_mats):
    widened, inv_rms, normed = normalize(in_rows, gain_row)
    picked, chosen, summed, probs = route_weights(normed, router_cols, route_ids)
    row_count = in_rows.shape[0]
    dnorm_all = jnp.zeros(in_rows.shape, jnp.float32)
    dprob_all = jnp.zeros(route_ids.shape, jnp.float32)
    limit = N_EXPERT * CAP
    for expert in range(EXPERTS):
        picked_rows, is_valid = expert_rows(route_ids, expert, limit)
        weight = lax.optimization_barrier(jnp.sum(picked[:, :, expert] * probs, axis=-1))[picked_rows] * is_valid
        dnormed, dprob = expert_backward(normed[picked_rows], grad_rows[picked_rows], gate_mats[expert], up_mats[expert], down_mats[expert])
        dnorm_all = dnorm_all.at[picked_rows].add(weight[:, None] * dnormed.astype(jnp.float32))
        dprob_rows = jnp.zeros((row_count,), jnp.float32).at[picked_rows].add(is_valid * dprob.astype(jnp.float32))
        dprob_all = dprob_all + picked[:, :, expert] * dprob_rows[:, None]
    return input_gradient(grad_rows, widened, inv_rms, gain_row, router_cols, picked, chosen, summed, probs, dnorm_all, dprob_all)

def reference(fwd_in, fwd_routes, saved_in, saved_routes, grad_in, norm_gain, router, w_gate, w_up, w_down):
    section_rows = TOK_DEV * N_EXPERT

    def one_section(section_args):
        f_rows, f_ids, s_rows, s_ids, g_rows, gain_row, router_cols, gate_mats, up_mats, down_mats = section_args
        forward = group_forward(f_rows, f_ids, gain_row, router_cols, gate_mats, up_mats, down_mats)
        backward = group_backward(s_rows, s_ids, g_rows, gain_row, router_cols, gate_mats, up_mats, down_mats)
        return (forward, backward)
    stacked = (fwd_in.reshape(N_PIPE, section_rows, D), fwd_routes.reshape(N_PIPE, section_rows, TOP), saved_in.reshape(N_PIPE, section_rows, D), saved_routes.reshape(N_PIPE, section_rows, TOP), grad_in.reshape(N_PIPE, section_rows, D), norm_gain, router, w_gate, w_up, w_down)
    forward_all, backward_all = lax.map(one_section, stacked)
    zero_block = jnp.zeros((1, section_rows, D), jnp.bfloat16)
    fwd_out = jnp.concatenate([zero_block, forward_all[:-1]], axis=0).reshape(TOKENS, D)
    grad_out = jnp.concatenate([backward_all[1:], zero_block], axis=0).reshape(TOKENS, D)
    return (fwd_out, grad_out)
```

```python
import functools

import jax
import jax.numpy as jnp
from jax import lax
from jax.experimental import pallas as pl
from jax.experimental.pallas import tpu as pltpu
from jax.sharding import PartitionSpec as P

EPSILON = 1e-06
MESH = pl.DeviceIdType.MESH
F32 = jnp.float32
BF16 = jnp.bfloat16
NT = (((1,), (1,)), ((), ()))
CHUNK = 32
STEP = 16


def kernel(
    n_pipe, tn, td,
    sx_hbm, z_hbm, fx_hbm, rt_in, gain, rout, wg_hbm, wu_hbm, wd_hbm,
    fo_hbm, go_hbm,
    sx, z, fx, rts, wg, wu, wd, rb, nrm, hh, dg, du, acc, cols, wb, wf, rcb, rcf, lpb, lpf, at, ar,
    loc_sem, w_sem, c_send, c_recv, l_send, l_recv, t_send, t_recv, pb_send, pb_recv, pf_send, pf_recv,
    go_send, go_recv, fo_send, fo_recv, zero_sem,
):
    c = lax.axis_index("pipe")
    e = lax.axis_index("expert")
    rows, width = sx_hbm.shape
    hidden = hh.shape[1]
    e_c = e + 1 - 2 * lax.rem(e, 2)
    e_l = lax.rem(e + 2, 4)
    e_d = lax.rem(e_c + 2, 4)
    core, link, diag = (c, e_c), (c, e_l), (c, e_d)
    after, before = (c + 1, e_l), (c - 1, e_l)
    n_chunks = rows // CHUNK

    def block(s):
        return pl.ds(s * rows, rows)

    def remote(src, dst, send, recv, to):
        return pltpu.make_async_remote_copy(
            src_ref=src, dst_ref=dst, send_sem=send, recv_sem=recv, device_id=to, device_id_type=MESH
        )

    def load_x(i):
        src, dst = ((sx_hbm, sx), (z_hbm, z), (fx_hbm, fx))[i]
        return pltpu.make_async_copy(src, dst.at[block(0)], loc_sem.at[i])

    def load_w(i, j):
        part = pl.ds(pl.multiple_of(j * tn, tn), tn)
        if i == 2:
            return pltpu.make_async_copy(wd_hbm.at[0, 0, part], wd.at[part], w_sem.at[i, j])
        src, dst = ((wg_hbm, wg), (wu_hbm, wu))[i]
        return pltpu.make_async_copy(src.at[0, 0, :, part], dst.at[:, part], w_sem.at[i, j])

    def own_to_core(i):
        src, dst = ((sx_hbm, sx), (z_hbm, z), (fx_hbm, fx))[i]
        return remote(src, dst.at[block(1)], c_send.at[i], c_recv.at[i], core)

    def own_to_link(i):
        src, dst = ((sx_hbm, sx), (z_hbm, z), (fx_hbm, fx))[i]
        return remote(src, dst.at[block(2)], l_send.at[i], l_recv.at[i], link)

    def pass_to_core(i):
        ref = (sx, z, fx)[i]
        return remote(ref.at[block(2)], ref.at[block(3)], c_send.at[3 + i], c_recv.at[3 + i], core)

    def sums_to_core(i, g):
        src, dst = ((wb, rcb), (wf, rcf))[i]
        k = 6 + 2 * i + g
        return remote(src.at[block(2 * g + 1)], dst.at[block(g)], c_send.at[k], c_recv.at[k], core)

    def routes_to(s):
        return remote(rt_in, rts.at[s], t_send.at[s - 1], t_recv.at[s - 1], (core, link, diag)[s - 1])

    def dots_to(s):
        t = (None, 3, 0, 1)[s]
        return remote(at.at[t], ar.at[s], t_send.at[2 + s], t_recv.at[2 + s], (core, link, diag)[s - 1])

    def part(q):
        return pl.ds(pl.multiple_of(q * CHUNK, CHUNK), CHUNK)

    def tail(q):
        return pl.ds(pl.multiple_of(2 * rows + q * CHUNK, CHUNK), CHUNK)

    def sums_to_link(i, q):
        src, dst, send, recv = ((wb, lpb, pb_send, pb_recv), (wf, lpf, pf_send, pf_recv))[i]
        return remote(src.at[part(q)], dst.at[part(q)], send.at[q], recv.at[q], link)

    def result(i, q):
        if i == 0:
            return remote(wb.at[tail(q)], go_hbm.at[part(q)], go_send.at[q], go_recv.at[q], before)
        return remote(wf.at[tail(q)], fo_hbm.at[part(q)], fo_send.at[q], fo_recv.at[q], after)

    tiles = hidden // tn
    load_x(0).start()
    for j in range(tiles):
        load_w(0, j).start()
        load_w(1, j).start()
        if j == 0:
            load_x(1).start()
        load_w(2, j).start()
    load_x(2).start()

    barrier = pltpu.get_barrier_semaphore()
    ring = [(lax.rem(c + by, n_pipe), e_l) for by in (1, n_pipe - 1)]
    for peer in (core, link, diag, *ring):
        pl.semaphore_signal(barrier, inc=1, device_id=peer, device_id_type=MESH)
    pl.semaphore_wait(barrier, 5)

    for s in (1, 2, 3):
        routes_to(s).start()
    for i in range(3):
        own_to_link(i).start()
        own_to_core(i).start()

    rts[0] = rt_in[...]
    rb[...] = jnp.zeros_like(rb)
    rb[0:16, :] = rout[...]
    eye = lax.broadcasted_iota(jnp.int32, (rows, rows), 0) == lax.broadcasted_iota(jnp.int32, (rows, rows), 1)

    def to_col(row):
        return jnp.sum(jnp.where(eye, row, 0.0), axis=1, keepdims=True)

    def to_row(col):
        return jnp.sum(jnp.where(eye, col, 0.0), axis=0, keepdims=True)

    def normalize(x_ref, g):
        def step(q, _):
            at_rows = pl.ds(pl.multiple_of(2 * g * rows + q * STEP, STEP), STEP)
            to_rows = pl.ds(pl.multiple_of(q * STEP, STEP), STEP)
            wide = x_ref[at_rows, :].astype(F32)
            inv = lax.rsqrt(jnp.mean(wide * wide, axis=1, keepdims=True) + EPSILON)
            nrm[to_rows, :] = (wide * inv * gain[...]).astype(BF16)
            return 0

        lax.fori_loop(0, 2 * rows // STEP, step, 0)

    def route_weights(g, kind):
        logits = lax.dot_general(nrm[...], rb[...], NT, preferred_element_type=F32)
        scores = jax.nn.sigmoid(logits)
        lane = lax.broadcasted_iota(jnp.int32, (rows, 128), 1).astype(F32)
        me = e.astype(F32)
        out = []
        for h in range(2):
            s = 2 * g + h
            tile = rts[s]
            first = 2 - 2 * kind
            r0, r1 = to_col(tile[first : first + 1, :]), to_col(tile[first + 1 : first + 2, :])
            mine = scores[h * rows : (h + 1) * rows, :]
            q0 = jnp.sum(jnp.where(lane == r0, mine, 0.0), axis=1, keepdims=True)
            q1 = jnp.sum(jnp.where(lane == r1, mine, 0.0), axis=1, keepdims=True)
            total = q0 + q1
            out.append(jnp.where(r0 == me, q0 / total, 0.0) + jnp.where(r1 == me, q1 / total, 0.0))
            if s == 2 and kind == 0:
                cols[...] = jnp.where(lane == 0.0, q0, jnp.where(lane == 1.0, q1, 0.0))
        return jnp.concatenate(out, axis=0)

    def backward(g, first):
        normalize(sx, g)
        weight = route_weights(g, 0)
        here = pl.ds(2 * g * rows, 2 * rows)

        def hidden_step(j, _):
            cut = pl.ds(pl.multiple_of(j * tn, tn), tn)
            if first:
                for i in range(3):
                    load_w(i, j).wait()
            gate = jnp.dot(nrm[...], wg[:, cut], preferred_element_type=F32)
            up = jnp.dot(nrm[...], wu[:, cut], preferred_element_type=F32)
            dhid = lax.dot_general(z[here, :], wd[cut, :], NT, preferred_element_type=F32)
            sig = jax.nn.sigmoid(gate)
            silu = gate * sig
            hh[:, cut] = (silu * up).astype(BF16)
            dg[:, cut] = (dhid * up * sig * (1.0 + gate * (1.0 - sig))).astype(BF16)
            du[:, cut] = (dhid * silu).astype(BF16)
            return 0

        lax.fori_loop(0, tiles, hidden_step, 0)
        acc[...] = jnp.zeros_like(acc)

        def model_step(j, _):
            cut = pl.ds(pl.multiple_of(j * td, td), td)
            out = jnp.dot(hh[...], wd[:, cut], preferred_element_type=F32).astype(BF16).astype(F32)
            prod = z[here, cut].astype(F32) * out
            folded = prod[:, 0:128]
            for k in range(1, td // 128):
                folded = folded + prod[:, k * 128 : (k + 1) * 128]
            acc[...] += folded
            dn = lax.dot_general(dg[...], wg[cut, :], NT, preferred_element_type=F32)
            dn = dn + lax.dot_general(du[...], wu[cut, :], NT, preferred_element_type=F32)
            wb[here, cut] = (weight * dn.astype(BF16).astype(F32)).astype(BF16)
            return 0

        lax.fori_loop(0, width // td, model_step, 0)
        dots = jnp.sum(acc[...], axis=1, keepdims=True).astype(BF16).astype(F32)
        for h in range(2):
            row = to_row(dots[h * rows : (h + 1) * rows, :])
            at[2 * g + h] = jnp.broadcast_to(row, (8, rows))

    def forward(g):
        normalize(fx, g)
        weight = route_weights(g, 1)
        here = pl.ds(2 * g * rows, 2 * rows)

        def hidden_step(j, _):
            cut = pl.ds(pl.multiple_of(j * tn, tn), tn)
            gate = jnp.dot(nrm[...], wg[:, cut], preferred_element_type=F32)
            up = jnp.dot(nrm[...], wu[:, cut], preferred_element_type=F32)
            hh[:, cut] = (gate * jax.nn.sigmoid(gate) * up).astype(BF16)
            return 0

        lax.fori_loop(0, tiles, hidden_step, 0)

        def model_step(j, _):
            cut = pl.ds(pl.multiple_of(j * td, td), td)
            out = jnp.dot(hh[...], wd[:, cut], preferred_element_type=F32).astype(BF16).astype(F32)
            wf[here, cut] = (weight * out).astype(BF16)
            return 0

        lax.fori_loop(0, width // td, model_step, 0)

    def chip_sums(i):
        keep, got = ((wb, rcb), (wf, rcf))[i]
        sums_to_core(i, 0).wait_recv()

        def step(q, _):
            keep[part(q), :] = (keep[part(q), :].astype(F32) + got[part(q), :].astype(F32)).astype(BF16)
            sums_to_link(i, q).start()
            return 0

        lax.fori_loop(0, n_chunks, step, 0)

    load_x(0).wait()
    load_x(1).wait()
    own_to_core(0).wait_recv()
    own_to_core(1).wait_recv()
    for s in (1, 2, 3):
        routes_to(s).wait_recv()
    backward(0, True)
    sums_to_core(0, 0).start()
    dots_to(2).start()
    dots_to(3).start()
    load_x(2).wait()
    own_to_core(2).wait_recv()
    own_to_link(0).wait_recv()
    pass_to_core(0).start()
    forward(0)
    sums_to_core(1, 0).start()
    chip_sums(0)
    own_to_link(1).wait_recv()
    pass_to_core(1).start()
    chip_sums(1)

    pass_to_core(0).wait_recv()
    pass_to_core(1).wait_recv()
    backward(1, False)
    sums_to_core(0, 1).start()
    dots_to(1).start()
    own_to_link(2).wait_recv()
    pass_to_core(2).start()
    pass_to_core(2).wait_recv()
    forward(1)
    sums_to_core(1, 1).start()
    nrm[0:rows, :] = jnp.zeros((rows, width), BF16)

    @pl.when(c == 0)
    def _():
        pltpu.make_async_copy(nrm.at[0:rows], fo_hbm, zero_sem.at[0]).start()

    @pl.when(c == n_pipe - 1)
    def _():
        pltpu.make_async_copy(nrm.at[0:rows], go_hbm, zero_sem.at[1]).start()

    for s in (1, 2, 3):
        dots_to(s).wait_recv()
    tile = rts[2]
    r0, r1 = to_col(tile[2:3, :]), to_col(tile[3:4, :])
    saved = cols[...]
    q0, q1 = saved[:, 0:1], saved[:, 1:2]
    total = q0 + q1
    a0, a1 = jnp.zeros((rows, 1), F32), jnp.zeros((rows, 1), F32)
    for s, owner in enumerate((e, e_c, e_l, e_d)):
        got = at[2] if s == 0 else ar[s]
        dot_col = to_col(got[0:1, :])
        a0 = a0 + jnp.where(r0 == owner.astype(F32), dot_col, 0.0)
        a1 = a1 + jnp.where(r1 == owner.astype(F32), dot_col, 0.0)
    mixed = a0 * (q0 / total) + a1 * (q1 / total)
    l0 = (a0 - mixed) / total * q0 * (1.0 - q0)
    l1 = (a1 - mixed) / total * q1 * (1.0 - q1)
    lane = lax.broadcasted_iota(jnp.int32, (rows, 128), 1).astype(F32)
    cols[...] = jnp.where(lane == r0, l0, 0.0) + jnp.where(lane == r1, l1, 0.0)
    sums_to_core(0, 1).wait_recv()

    def finish_backward(q, _):
        sums_to_link(0, q).wait_recv()
        for k in range(CHUNK // STEP):
            at_rows = pl.ds(pl.multiple_of(q * CHUNK + k * STEP, STEP), STEP)
            far = pl.ds(pl.multiple_of(2 * rows + q * CHUNK + k * STEP, STEP), STEP)
            near = pl.ds(pl.multiple_of(rows + q * CHUNK + k * STEP, STEP), STEP)
            wide = sx[far, :].astype(F32)
            inv = lax.rsqrt(jnp.mean(wide * wide, axis=1, keepdims=True) + EPSILON)
            dn = wb[far, :].astype(F32) + rcb[near, :].astype(F32) + lpb[at_rows, :].astype(F32)
            lcol = cols[at_rows, :]
            for j in range(4):
                dn = dn + lcol[:, j : j + 1] * rout[j : j + 1, :].astype(F32)
            scaled = dn * gain[...]
            mean = jnp.mean(scaled * wide, axis=1, keepdims=True)
            grad = z[far, :].astype(F32) + (inv * scaled - wide * (inv * inv * inv * mean))
            wb[far, :] = grad.astype(BF16)

        @pl.when(c > 0)
        def _():
            result(0, q).start()

        return 0

    lax.fori_loop(0, n_chunks, finish_backward, 0)
    sums_to_core(1, 1).wait_recv()

    def finish_forward(q, _):
        sums_to_link(1, q).wait_recv()
        for k in range(CHUNK // STEP):
            at_rows = pl.ds(pl.multiple_of(q * CHUNK + k * STEP, STEP), STEP)
            far = pl.ds(pl.multiple_of(2 * rows + q * CHUNK + k * STEP, STEP), STEP)
            near = pl.ds(pl.multiple_of(rows + q * CHUNK + k * STEP, STEP), STEP)
            out = wf[far, :].astype(F32) + rcf[near, :].astype(F32) + lpf[at_rows, :].astype(F32)
            wf[far, :] = (fx[far, :].astype(F32) + out).astype(BF16)

        @pl.when(c < n_pipe - 1)
        def _():
            result(1, q).start()

        return 0

    lax.fori_loop(0, n_chunks, finish_forward, 0)

    for s in (1, 2, 3):
        routes_to(s).wait_send()
        dots_to(s).wait_send()
    for i in range(3):
        own_to_core(i).wait_send()
        own_to_link(i).wait_send()
        pass_to_core(i).wait_send()
    for i in range(2):
        for g in range(2):
            sums_to_core(i, g).wait_send()
        for q in range(n_chunks):
            sums_to_link(i, q).wait_send()

    @pl.when(c > 0)
    def _():
        for q in range(n_chunks):
            result(0, q).wait_send()
            result(1, q).wait_recv()

    @pl.when(c < n_pipe - 1)
    def _():
        for q in range(n_chunks):
            result(1, q).wait_send()
            result(0, q).wait_recv()

    @pl.when(c == 0)
    def _():
        pltpu.make_async_copy(nrm.at[0:rows], fo_hbm, zero_sem.at[0]).wait()

    @pl.when(c == n_pipe - 1)
    def _():
        pltpu.make_async_copy(nrm.at[0:rows], go_hbm, zero_sem.at[1]).wait()


def local(
    n_pipe, fwd_in, fwd_routes, saved_in, saved_routes, grad_in, norm_gain, router, w_gate, w_up, w_down
):
    rows, width = fwd_in.shape
    hidden = w_gate.shape[3]
    tn = min(256, hidden)
    td = 512 if width % 512 == 0 else 128
    routes = jnp.concatenate([fwd_routes.T, saved_routes.T, fwd_routes.T, saved_routes.T], axis=0).astype(F32)
    rout = jnp.pad(router[0].T, ((0, 12), (0, 0)))
    n_chunks = rows // CHUNK
    dma = pltpu.SemaphoreType.DMA
    vmem = pl.BlockSpec(memory_space=pltpu.VMEM)
    hbm = pl.BlockSpec(memory_space=pl.ANY)
    grad_out_type = jax.ShapeDtypeStruct((rows, width), BF16)
    fwd_out, grad_out = pl.pallas_call(
        functools.partial(kernel, n_pipe, tn, td),
        out_shape=(grad_out_type, grad_out_type),
        in_specs=[hbm, hbm, hbm, vmem, vmem, vmem, hbm, hbm, hbm],
        out_specs=(hbm, hbm),
        scratch_shapes=[
            pltpu.VMEM((4 * rows, width), BF16),
            pltpu.VMEM((4 * rows, width), BF16),
            pltpu.VMEM((4 * rows, width), BF16),
            pltpu.VMEM((4, 8, rows), F32),
            pltpu.VMEM((width, hidden), BF16),
            pltpu.VMEM((width, hidden), BF16),
            pltpu.VMEM((hidden, width), BF16),
            pltpu.VMEM((128, width), BF16),
            pltpu.VMEM((2 * rows, width), BF16),
            pltpu.VMEM((2 * rows, hidden), BF16),
            pltpu.VMEM((2 * rows, hidden), BF16),
            pltpu.VMEM((2 * rows, hidden), BF16),
            pltpu.VMEM((2 * rows, 128), F32),
            pltpu.VMEM((rows, 128), F32),
            pltpu.VMEM((4 * rows, width), BF16),
            pltpu.VMEM((4 * rows, width), BF16),
            pltpu.VMEM((2 * rows, width), BF16),
            pltpu.VMEM((2 * rows, width), BF16),
            pltpu.VMEM((rows, width), BF16),
            pltpu.VMEM((rows, width), BF16),
            pltpu.VMEM((4, 8, rows), F32),
            pltpu.VMEM((4, 8, rows), F32),
            dma((3,)), dma((3, hidden // tn)),
            dma((10,)), dma((10,)),
            dma((3,)), dma((3,)),
            dma((6,)), dma((6,)),
            dma((n_chunks,)), dma((n_chunks,)),
            dma((n_chunks,)), dma((n_chunks,)),
            dma((n_chunks,)), dma((n_chunks,)),
            dma((n_chunks,)), dma((n_chunks,)),
            dma((2,)),
        ],
        compiler_params=pltpu.CompilerParams(
            collective_id=0, has_side_effects=True, vmem_limit_bytes=67043328
        ),
        name="relay_slot",
    )(saved_in, grad_in, fwd_in, routes, norm_gain, rout, w_gate, w_up, w_down)
    return fwd_out, grad_out


def solution(mesh):
    rows = P(("pipe", "expert"), None)
    in_specs = (
        rows, rows, rows, rows, rows,
        P("pipe", None),
        P("pipe", None, None),
        P("pipe", "expert", None, None),
        P("pipe", "expert", None, None),
        P("pipe", "expert", None, None),
    )
    return jax.shard_map(
        functools.partial(local, mesh.shape["pipe"]),
        mesh=mesh, in_specs=in_specs, out_specs=(rows, rows), check_vma=False,
    )
```

```python
import functools

import jax
import jax.numpy as jnp
from jax import lax
from jax.experimental import pallas as pl
from jax.experimental.pallas import tpu as pltpu
from jax.sharding import PartitionSpec as P

EPSILON = 1e-06
MESH = pl.DeviceIdType.MESH
F32 = jnp.float32
BF16 = jnp.bfloat16
NT = (((1,), (1,)), ((), ()))
CHUNK = 16
STEP = 16


def kernel(
    n_pipe, tn, td,
    sx_hbm, z_hbm, fx_hbm, rt_in, gain, rout, wg_hbm, wu_hbm, wd_hbm,
    fo_hbm, go_hbm,
    sx, z, fx, rts, wg, wu, wd, rb, nrm, hh, dg, du, acc, cols, wb, wf, rcb, rcf, lpb, lpf, at, ar,
    loc_sem, w_sem, c_send, c_recv, l_send, l_recv, t_send, t_recv, pb_send, pb_recv, pf_send, pf_recv,
    go_send, go_recv, fo_send, fo_recv, zero_sem,
):
    c = lax.axis_index("pipe")
    e = lax.axis_index("expert")
    rows, width = sx_hbm.shape
    hidden = hh.shape[1]
    e_c = e + 1 - 2 * lax.rem(e, 2)
    e_l = lax.rem(e + 2, 4)
    e_d = lax.rem(e_c + 2, 4)
    core, link, diag = (c, e_c), (c, e_l), (c, e_d)
    after, before = (c + 1, e_l), (c - 1, e_l)
    n_chunks = rows // CHUNK

    def block(s):
        return pl.ds(s * rows, rows)

    def remote(src, dst, send, recv, to):
        return pltpu.make_async_remote_copy(
            src_ref=src, dst_ref=dst, send_sem=send, recv_sem=recv, device_id=to, device_id_type=MESH
        )

    def load_x(i):
        src, dst = ((sx_hbm, sx), (z_hbm, z), (fx_hbm, fx))[i]
        return pltpu.make_async_copy(src, dst.at[block(0)], loc_sem.at[i])

    def load_w(i, j):
        part = pl.ds(pl.multiple_of(j * tn, tn), tn)
        if i == 2:
            return pltpu.make_async_copy(wd_hbm.at[0, 0, part], wd.at[part], w_sem.at[i, j])
        src, dst = ((wg_hbm, wg), (wu_hbm, wu))[i]
        return pltpu.make_async_copy(src.at[0, 0, :, part], dst.at[:, part], w_sem.at[i, j])

    def own_to_core(i):
        src, dst = ((sx_hbm, sx), (z_hbm, z), (fx_hbm, fx))[i]
        return remote(src, dst.at[block(1)], c_send.at[i], c_recv.at[i], core)

    def own_to_link(i):
        src, dst = ((sx_hbm, sx), (z_hbm, z), (fx_hbm, fx))[i]
        return remote(src, dst.at[block(2)], l_send.at[i], l_recv.at[i], link)

    def pass_to_core(i):
        ref = (sx, z, fx)[i]
        return remote(ref.at[block(2)], ref.at[block(3)], c_send.at[3 + i], c_recv.at[3 + i], core)

    def sums_to_core(i, g):
        src, dst = ((wb, rcb), (wf, rcf))[i]
        k = 6 + 2 * i + g
        return remote(src.at[block(2 * g + 1)], dst.at[block(g)], c_send.at[k], c_recv.at[k], core)

    def routes_to(s):
        return remote(rt_in, rts.at[s], t_send.at[s - 1], t_recv.at[s - 1], (core, link, diag)[s - 1])

    def dots_to(s):
        t = (None, 3, 0, 1)[s]
        return remote(at.at[t], ar.at[s], t_send.at[2 + s], t_recv.at[2 + s], (core, link, diag)[s - 1])

    def part(q):
        return pl.ds(pl.multiple_of(q * CHUNK, CHUNK), CHUNK)

    def tail(q):
        return pl.ds(pl.multiple_of(2 * rows + q * CHUNK, CHUNK), CHUNK)

    def sums_to_link(i, q):
        src, dst, send, recv = ((wb, lpb, pb_send, pb_recv), (wf, lpf, pf_send, pf_recv))[i]
        return remote(src.at[part(q)], dst.at[part(q)], send.at[q], recv.at[q], link)

    def result(i, q):
        if i == 0:
            return remote(wb.at[tail(q)], go_hbm.at[part(q)], go_send.at[q], go_recv.at[q], before)
        return remote(wf.at[tail(q)], fo_hbm.at[part(q)], fo_send.at[q], fo_recv.at[q], after)

    tiles = hidden // tn
    load_x(0).start()
    for j in range(tiles):
        load_w(0, j).start()
        load_w(1, j).start()
        if j == 0:
            load_x(1).start()
        load_w(2, j).start()
    load_x(2).start()

    barrier = pltpu.get_barrier_semaphore()
    ring = [(lax.rem(c + by, n_pipe), e_l) for by in (1, n_pipe - 1)]
    for peer in (core, link, diag, *ring):
        pl.semaphore_signal(barrier, inc=1, device_id=peer, device_id_type=MESH)
    pl.semaphore_wait(barrier, 5)

    for s in (1, 2, 3):
        routes_to(s).start()
    for i in range(3):
        own_to_link(i).start()
        own_to_core(i).start()

    rts[0] = rt_in[...]
    rb[...] = jnp.zeros_like(rb)
    rb[0:16, :] = rout[...]
    eye = lax.broadcasted_iota(jnp.int32, (rows, rows), 0) == lax.broadcasted_iota(jnp.int32, (rows, rows), 1)

    def to_col(row):
        return jnp.sum(jnp.where(eye, row, 0.0), axis=1, keepdims=True)

    def to_row(col):
        return jnp.sum(jnp.where(eye, col, 0.0), axis=0, keepdims=True)

    def normalize(x_ref, g):
        def step(q, _):
            at_rows = pl.ds(pl.multiple_of(2 * g * rows + q * STEP, STEP), STEP)
            to_rows = pl.ds(pl.multiple_of(q * STEP, STEP), STEP)
            wide = x_ref[at_rows, :].astype(F32)
            inv = lax.rsqrt(jnp.mean(wide * wide, axis=1, keepdims=True) + EPSILON)
            nrm[to_rows, :] = (wide * inv * gain[...]).astype(BF16)
            return 0

        lax.fori_loop(0, 2 * rows // STEP, step, 0)

    def route_weights(g, kind):
        logits = lax.dot_general(nrm[...], rb[...], NT, preferred_element_type=F32)
        scores = jax.nn.sigmoid(logits)
        lane = lax.broadcasted_iota(jnp.int32, (rows, 128), 1).astype(F32)
        me = e.astype(F32)
        out = []
        for h in range(2):
            s = 2 * g + h
            tile = rts[s]
            first = 2 - 2 * kind
            r0, r1 = to_col(tile[first : first + 1, :]), to_col(tile[first + 1 : first + 2, :])
            mine = scores[h * rows : (h + 1) * rows, :]
            q0 = jnp.sum(jnp.where(lane == r0, mine, 0.0), axis=1, keepdims=True)
            q1 = jnp.sum(jnp.where(lane == r1, mine, 0.0), axis=1, keepdims=True)
            total = q0 + q1
            out.append(jnp.where(r0 == me, q0 / total, 0.0) + jnp.where(r1 == me, q1 / total, 0.0))
            if s == 2 and kind == 0:
                cols[...] = jnp.where(lane == 0.0, q0, jnp.where(lane == 1.0, q1, 0.0))
        return jnp.concatenate(out, axis=0)

    def backward(g, first):
        normalize(sx, g)
        weight = route_weights(g, 0)
        here = pl.ds(2 * g * rows, 2 * rows)

        def hidden_step(j, _):
            cut = pl.ds(pl.multiple_of(j * tn, tn), tn)
            if first:
                for i in range(3):
                    load_w(i, j).wait()
            gate = jnp.dot(nrm[...], wg[:, cut], preferred_element_type=F32)
            up = jnp.dot(nrm[...], wu[:, cut], preferred_element_type=F32)
            dhid = lax.dot_general(z[here, :], wd[cut, :], NT, preferred_element_type=F32)
            sig = jax.nn.sigmoid(gate)
            silu = gate * sig
            hh[:, cut] = (silu * up).astype(BF16)
            dg[:, cut] = (dhid * up * sig * (1.0 + gate * (1.0 - sig))).astype(BF16)
            du[:, cut] = (dhid * silu).astype(BF16)
            return 0

        lax.fori_loop(0, tiles, hidden_step, 0)
        acc[...] = jnp.zeros_like(acc)

        def model_step(j, _):
            cut = pl.ds(pl.multiple_of(j * td, td), td)
            out = jnp.dot(hh[...], wd[:, cut], preferred_element_type=F32).astype(BF16).astype(F32)
            prod = z[here, cut].astype(F32) * out
            folded = prod[:, 0:128]
            for k in range(1, td // 128):
                folded = folded + prod[:, k * 128 : (k + 1) * 128]
            acc[...] += folded
            dn = lax.dot_general(dg[...], wg[cut, :], NT, preferred_element_type=F32)
            dn = dn + lax.dot_general(du[...], wu[cut, :], NT, preferred_element_type=F32)
            wb[here, cut] = (weight * dn.astype(BF16).astype(F32)).astype(BF16)
            return 0

        lax.fori_loop(0, width // td, model_step, 0)
        dots = jnp.sum(acc[...], axis=1, keepdims=True).astype(BF16).astype(F32)
        for h in range(2):
            row = to_row(dots[h * rows : (h + 1) * rows, :])
            at[2 * g + h] = jnp.broadcast_to(row, (8, rows))

    def forward(g, between=None):
        normalize(fx, g)
        weight = route_weights(g, 1)
        here = pl.ds(2 * g * rows, 2 * rows)

        def hidden_step(j, _):
            cut = pl.ds(pl.multiple_of(j * tn, tn), tn)
            gate = jnp.dot(nrm[...], wg[:, cut], preferred_element_type=F32)
            up = jnp.dot(nrm[...], wu[:, cut], preferred_element_type=F32)
            hh[:, cut] = (gate * jax.nn.sigmoid(gate) * up).astype(BF16)
            if between is not None:
                between(j)
            return 0

        lax.fori_loop(0, tiles, hidden_step, 0)

        def model_step(j, _):
            cut = pl.ds(pl.multiple_of(j * td, td), td)
            out = jnp.dot(hh[...], wd[:, cut], preferred_element_type=F32).astype(BF16).astype(F32)
            wf[here, cut] = (weight * out).astype(BF16)
            return 0

        lax.fori_loop(0, width // td, model_step, 0)

    def chip_sums(i):
        keep, got = ((wb, rcb), (wf, rcf))[i]
        sums_to_core(i, 0).wait_recv()

        def step(q, _):
            keep[part(q), :] = (keep[part(q), :].astype(F32) + got[part(q), :].astype(F32)).astype(BF16)
            sums_to_link(i, q).start()
            return 0

        lax.fori_loop(0, n_chunks, step, 0)

    load_x(0).wait()
    load_x(1).wait()
    own_to_core(0).wait_recv()
    own_to_core(1).wait_recv()
    for s in (1, 2, 3):
        routes_to(s).wait_recv()
    backward(0, True)
    sums_to_core(0, 0).start()
    dots_to(2).start()
    dots_to(3).start()
    load_x(2).wait()
    own_to_core(2).wait_recv()
    own_to_link(0).wait_recv()
    pass_to_core(0).start()
    forward(0)
    sums_to_core(1, 0).start()
    chip_sums(0)
    own_to_link(1).wait_recv()
    pass_to_core(1).start()
    chip_sums(1)

    pass_to_core(0).wait_recv()
    pass_to_core(1).wait_recv()
    backward(1, False)
    sums_to_core(0, 1).start()
    dots_to(1).start()
    own_to_link(2).wait_recv()
    pass_to_core(2).start()
    for s in (1, 2, 3):
        dots_to(s).wait_recv()
    tile = rts[2]
    r0, r1 = to_col(tile[2:3, :]), to_col(tile[3:4, :])
    saved = cols[...]
    q0, q1 = saved[:, 0:1], saved[:, 1:2]
    total = q0 + q1
    a0, a1 = jnp.zeros((rows, 1), F32), jnp.zeros((rows, 1), F32)
    for s, owner in enumerate((e, e_c, e_l, e_d)):
        got = at[2] if s == 0 else ar[s]
        dot_col = to_col(got[0:1, :])
        a0 = a0 + jnp.where(r0 == owner.astype(F32), dot_col, 0.0)
        a1 = a1 + jnp.where(r1 == owner.astype(F32), dot_col, 0.0)
    mixed = a0 * (q0 / total) + a1 * (q1 / total)
    l0 = (a0 - mixed) / total * q0 * (1.0 - q0)
    l1 = (a1 - mixed) / total * q1 * (1.0 - q1)
    lane = lax.broadcasted_iota(jnp.int32, (rows, 128), 1).astype(F32)
    cols[...] = jnp.where(lane == r0, l0, 0.0) + jnp.where(lane == r1, l1, 0.0)
    sums_to_core(0, 1).wait_recv()

    def finish_backward(q, _):
        sums_to_link(0, q).wait_recv()
        for k in range(CHUNK // STEP):
            at_rows = pl.ds(pl.multiple_of(q * CHUNK + k * STEP, STEP), STEP)
            far = pl.ds(pl.multiple_of(2 * rows + q * CHUNK + k * STEP, STEP), STEP)
            near = pl.ds(pl.multiple_of(rows + q * CHUNK + k * STEP, STEP), STEP)
            wide = sx[far, :].astype(F32)
            inv = lax.rsqrt(jnp.mean(wide * wide, axis=1, keepdims=True) + EPSILON)
            dn = wb[far, :].astype(F32) + rcb[near, :].astype(F32) + lpb[at_rows, :].astype(F32)
            lcol = cols[at_rows, :]
            for j in range(4):
                dn = dn + lcol[:, j : j + 1] * rout[j : j + 1, :].astype(F32)
            scaled = dn * gain[...]
            mean = jnp.mean(scaled * wide, axis=1, keepdims=True)
            grad = z[far, :].astype(F32) + (inv * scaled - wide * (inv * inv * inv * mean))
            wb[far, :] = grad.astype(BF16)

        @pl.when(c > 0)
        def _():
            result(0, q).start()

        return 0

    early = n_chunks - tiles - 2
    lax.fori_loop(0, early, finish_backward, 0)
    pass_to_core(2).wait_recv()
    forward(1, lambda j: finish_backward(early + j, 0))
    sums_to_core(1, 1).start()
    lax.fori_loop(early + tiles, n_chunks, finish_backward, 0)
    nrm[0:rows, :] = jnp.zeros((rows, width), BF16)

    @pl.when(c == 0)
    def _():
        pltpu.make_async_copy(nrm.at[0:rows], fo_hbm, zero_sem.at[0]).start()

    @pl.when(c == n_pipe - 1)
    def _():
        pltpu.make_async_copy(nrm.at[0:rows], go_hbm, zero_sem.at[1]).start()

    sums_to_core(1, 1).wait_recv()

    def finish_forward(q, _):
        sums_to_link(1, q).wait_recv()
        for k in range(CHUNK // STEP):
            at_rows = pl.ds(pl.multiple_of(q * CHUNK + k * STEP, STEP), STEP)
            far = pl.ds(pl.multiple_of(2 * rows + q * CHUNK + k * STEP, STEP), STEP)
            near = pl.ds(pl.multiple_of(rows + q * CHUNK + k * STEP, STEP), STEP)
            out = wf[far, :].astype(F32) + rcf[near, :].astype(F32) + lpf[at_rows, :].astype(F32)
            wf[far, :] = (fx[far, :].astype(F32) + out).astype(BF16)

        @pl.when(c < n_pipe - 1)
        def _():
            result(1, q).start()

        return 0

    lax.fori_loop(0, n_chunks, finish_forward, 0)

    for s in (1, 2, 3):
        routes_to(s).wait_send()
        dots_to(s).wait_send()
    for i in range(3):
        own_to_core(i).wait_send()
        own_to_link(i).wait_send()
        pass_to_core(i).wait_send()
    for i in range(2):
        for g in range(2):
            sums_to_core(i, g).wait_send()
        for q in range(n_chunks):
            sums_to_link(i, q).wait_send()

    @pl.when(c > 0)
    def _():
        for q in range(n_chunks):
            result(0, q).wait_send()
            result(1, q).wait_recv()

    @pl.when(c < n_pipe - 1)
    def _():
        for q in range(n_chunks):
            result(1, q).wait_send()
            result(0, q).wait_recv()

    @pl.when(c == 0)
    def _():
        pltpu.make_async_copy(nrm.at[0:rows], fo_hbm, zero_sem.at[0]).wait()

    @pl.when(c == n_pipe - 1)
    def _():
        pltpu.make_async_copy(nrm.at[0:rows], go_hbm, zero_sem.at[1]).wait()


def local(
    n_pipe, fwd_in, fwd_routes, saved_in, saved_routes, grad_in, norm_gain, router, w_gate, w_up, w_down
):
    rows, width = fwd_in.shape
    hidden = w_gate.shape[3]
    tn = min(256, hidden)
    td = 512 if width % 512 == 0 else 128
    routes = jnp.concatenate([fwd_routes.T, saved_routes.T, fwd_routes.T, saved_routes.T], axis=0).astype(F32)
    rout = jnp.pad(router[0].T, ((0, 12), (0, 0)))
    n_chunks = rows // CHUNK
    dma = pltpu.SemaphoreType.DMA
    vmem = pl.BlockSpec(memory_space=pltpu.VMEM)
    hbm = pl.BlockSpec(memory_space=pl.ANY)
    grad_out_type = jax.ShapeDtypeStruct((rows, width), BF16)
    fwd_out, grad_out = pl.pallas_call(
        functools.partial(kernel, n_pipe, tn, td),
        out_shape=(grad_out_type, grad_out_type),
        in_specs=[hbm, hbm, hbm, vmem, vmem, vmem, hbm, hbm, hbm],
        out_specs=(hbm, hbm),
        scratch_shapes=[
            pltpu.VMEM((4 * rows, width), BF16),
            pltpu.VMEM((4 * rows, width), BF16),
            pltpu.VMEM((4 * rows, width), BF16),
            pltpu.VMEM((4, 8, rows), F32),
            pltpu.VMEM((width, hidden), BF16),
            pltpu.VMEM((width, hidden), BF16),
            pltpu.VMEM((hidden, width), BF16),
            pltpu.VMEM((128, width), BF16),
            pltpu.VMEM((2 * rows, width), BF16),
            pltpu.VMEM((2 * rows, hidden), BF16),
            pltpu.VMEM((2 * rows, hidden), BF16),
            pltpu.VMEM((2 * rows, hidden), BF16),
            pltpu.VMEM((2 * rows, 128), F32),
            pltpu.VMEM((rows, 128), F32),
            pltpu.VMEM((4 * rows, width), BF16),
            pltpu.VMEM((4 * rows, width), BF16),
            pltpu.VMEM((2 * rows, width), BF16),
            pltpu.VMEM((2 * rows, width), BF16),
            pltpu.VMEM((rows, width), BF16),
            pltpu.VMEM((rows, width), BF16),
            pltpu.VMEM((4, 8, rows), F32),
            pltpu.VMEM((4, 8, rows), F32),
            dma((3,)), dma((3, hidden // tn)),
            dma((10,)), dma((10,)),
            dma((3,)), dma((3,)),
            dma((6,)), dma((6,)),
            dma((n_chunks,)), dma((n_chunks,)),
            dma((n_chunks,)), dma((n_chunks,)),
            dma((n_chunks,)), dma((n_chunks,)),
            dma((n_chunks,)), dma((n_chunks,)),
            dma((2,)),
        ],
        compiler_params=pltpu.CompilerParams(
            collective_id=0, has_side_effects=True, vmem_limit_bytes=67043328
        ),
        name="relay_slot",
    )(saved_in, grad_in, fwd_in, routes, norm_gain, rout, w_gate, w_up, w_down)
    return fwd_out, grad_out


def solution(mesh):
    rows = P(("pipe", "expert"), None)
    in_specs = (
        rows, rows, rows, rows, rows,
        P("pipe", None),
        P("pipe", None, None),
        P("pipe", "expert", None, None),
        P("pipe", "expert", None, None),
        P("pipe", "expert", None, None),
    )
    return jax.shard_map(
        functools.partial(local, mesh.shape["pipe"]),
        mesh=mesh, in_specs=in_specs, out_specs=(rows, rows), check_vma=False,
    )
```

```python
import functools

import jax
import jax.numpy as jnp
from jax import lax
from jax.experimental import pallas as pl
from jax.experimental.pallas import tpu as pltpu
from jax.sharding import PartitionSpec as P

EPSILON = 1e-06
MESH = pl.DeviceIdType.MESH
F32 = jnp.float32
BF16 = jnp.bfloat16
NT = (((1,), (1,)), ((), ()))
CHUNK = 16
STEP = 16


def kernel(
    n_pipe, tn, td,
    sx_hbm, z_hbm, fx_hbm, rt_s, rt_f, gain, rout, wg_hbm, wu_hbm, wd_hbm,
    fo_hbm, go_hbm,
    sx, z, fx, rts, wg, wu, wd, rb, nrm, hh, dg, du, acc, cols, wb, wf, rcb, rcf, lpb, lpf, at, ar,
    loc_sem, w_sem, c_send, c_recv, l_send, l_recv, r_send, r_recv, t_send, t_recv, pb_send, pb_recv, pf_send, pf_recv,
    go_send, go_recv, fo_send, fo_recv, zero_sem,
):
    c = lax.axis_index("pipe")
    e = lax.axis_index("expert")
    rows, width = sx_hbm.shape
    hidden = hh.shape[1]
    e_c = e + 1 - 2 * lax.rem(e, 2)
    e_l = lax.rem(e + 2, 4)
    e_d = lax.rem(e_c + 2, 4)
    core, link, diag = (c, e_c), (c, e_l), (c, e_d)
    after, before = (c + 1, e_l), (c - 1, e_l)
    n_chunks = rows // CHUNK

    def block(s):
        return pl.ds(s * rows, rows)

    def remote(src, dst, send, recv, to):
        return pltpu.make_async_remote_copy(
            src_ref=src, dst_ref=dst, send_sem=send, recv_sem=recv, device_id=to, device_id_type=MESH
        )

    def load_x(i):
        src, dst = ((sx_hbm, sx), (z_hbm, z), (fx_hbm, fx))[i]
        return pltpu.make_async_copy(src, dst.at[block(0)], loc_sem.at[i])

    def load_w(i, j):
        part = pl.ds(pl.multiple_of(j * tn, tn), tn)
        if i == 2:
            return pltpu.make_async_copy(wd_hbm.at[0, 0, part], wd.at[part], w_sem.at[i, j])
        src, dst = ((wg_hbm, wg), (wu_hbm, wu))[i]
        return pltpu.make_async_copy(src.at[0, 0, :, part], dst.at[:, part], w_sem.at[i, j])

    def own_to_core(i):
        src, dst = ((sx_hbm, sx), (z_hbm, z), (fx_hbm, fx))[i]
        return remote(src, dst.at[block(1)], c_send.at[i], c_recv.at[i], core)

    def own_to_link(i):
        src, dst = ((sx_hbm, sx), (z_hbm, z), (fx_hbm, fx))[i]
        return remote(src, dst.at[block(2)], l_send.at[i], l_recv.at[i], link)

    def pass_to_core(i):
        ref = (sx, z, fx)[i]
        return remote(ref.at[block(2)], ref.at[block(3)], c_send.at[3 + i], c_recv.at[3 + i], core)

    def sums_to_core(i, g):
        src, dst = ((wb, rcb), (wf, rcf))[i]
        k = 6 + 2 * i + g
        return remote(src.at[block(2 * g + 1)], dst.at[block(g)], c_send.at[k], c_recv.at[k], core)

    def routes_to(s, kind):
        k = 3 * kind + s - 1
        return remote((rt_s, rt_f)[kind], rts.at[kind, s], r_send.at[k], r_recv.at[k], (core, link, diag)[s - 1])

    def dots_to(s):
        t = (None, 3, 0, 1)[s]
        return remote(at.at[t], ar.at[s], t_send.at[s - 1], t_recv.at[s - 1], (core, link, diag)[s - 1])

    def part(q):
        return pl.ds(pl.multiple_of(q * CHUNK, CHUNK), CHUNK)

    def tail(q):
        return pl.ds(pl.multiple_of(2 * rows + q * CHUNK, CHUNK), CHUNK)

    def sums_to_link(i, q):
        src, dst, send, recv = ((wb, lpb, pb_send, pb_recv), (wf, lpf, pf_send, pf_recv))[i]
        return remote(src.at[part(q)], dst.at[part(q)], send.at[q], recv.at[q], link)

    def result(i, q):
        if i == 0:
            return remote(wb.at[tail(q)], go_hbm.at[part(q)], go_send.at[q], go_recv.at[q], before)
        return remote(wf.at[tail(q)], fo_hbm.at[part(q)], fo_send.at[q], fo_recv.at[q], after)

    tiles = hidden // tn
    load_x(0).start()
    for j in range(tiles):
        load_w(0, j).start()
        load_w(1, j).start()
        if j == 0:
            load_x(1).start()
        load_w(2, j).start()
    load_x(2).start()

    barrier = pltpu.get_barrier_semaphore()
    ring = [(lax.rem(c + by, n_pipe), e_l) for by in (1, n_pipe - 1)]
    for peer in (core, link, diag, *ring):
        pl.semaphore_signal(barrier, inc=1, device_id=peer, device_id_type=MESH)
    pl.semaphore_wait(barrier, 5)

    for s in (1, 2, 3):
        routes_to(s, 0).start()
        routes_to(s, 1).start()
    for i in range(3):
        own_to_link(i).start()
        own_to_core(i).start()

    rts[0, 0] = rt_s[...]
    rts[1, 0] = rt_f[...]
    rb[...] = jnp.zeros_like(rb)
    table = rout[...].astype(F32)
    rb[0:16, :] = jnp.concatenate([table, jnp.zeros((12, width), F32)], axis=0).astype(BF16)
    eye = lax.broadcasted_iota(jnp.int32, (rows, rows), 0) == lax.broadcasted_iota(jnp.int32, (rows, rows), 1)

    def to_col(row):
        return jnp.sum(jnp.where(eye, row, 0.0), axis=1, keepdims=True)

    def to_row(col):
        return jnp.sum(jnp.where(eye, col, 0.0), axis=0, keepdims=True)

    def normalize(x_ref, g):
        def step(q, _):
            at_rows = pl.ds(pl.multiple_of(2 * g * rows + q * STEP, STEP), STEP)
            to_rows = pl.ds(pl.multiple_of(q * STEP, STEP), STEP)
            wide = x_ref[at_rows, :].astype(F32)
            inv = lax.rsqrt(jnp.mean(wide * wide, axis=1, keepdims=True) + EPSILON)
            nrm[to_rows, :] = (wide * inv * gain[...]).astype(BF16)
            return 0

        lax.fori_loop(0, 2 * rows // STEP, step, 0)

    def route_weights(g, kind):
        logits = lax.dot_general(nrm[...], rb[...], NT, preferred_element_type=F32)
        scores = jax.nn.sigmoid(logits)
        lane = lax.broadcasted_iota(jnp.int32, (rows, 128), 1).astype(F32)
        me = e.astype(F32)
        out = []
        for h in range(2):
            s = 2 * g + h
            tile = rts[kind, s].astype(F32)
            r0, r1 = to_col(tile[0:1, :]), to_col(tile[1:2, :])
            mine = scores[h * rows : (h + 1) * rows, :]
            q0 = jnp.sum(jnp.where(lane == r0, mine, 0.0), axis=1, keepdims=True)
            q1 = jnp.sum(jnp.where(lane == r1, mine, 0.0), axis=1, keepdims=True)
            total = q0 + q1
            out.append(jnp.where(r0 == me, q0 / total, 0.0) + jnp.where(r1 == me, q1 / total, 0.0))
            if s == 2 and kind == 0:
                cols[...] = jnp.where(lane == 0.0, q0, jnp.where(lane == 1.0, q1, 0.0))
        return jnp.concatenate(out, axis=0)

    def backward(g, first):
        normalize(sx, g)
        weight = route_weights(g, 0)
        here = pl.ds(2 * g * rows, 2 * rows)

        def hidden_step(j, _):
            cut = pl.ds(pl.multiple_of(j * tn, tn), tn)
            if first:
                for i in range(3):
                    load_w(i, j).wait()
            gate = jnp.dot(nrm[...], wg[:, cut], preferred_element_type=F32)
            up = jnp.dot(nrm[...], wu[:, cut], preferred_element_type=F32)
            dhid = lax.dot_general(z[here, :], wd[cut, :], NT, preferred_element_type=F32)
            sig = jax.nn.sigmoid(gate)
            silu = gate * sig
            hh[:, cut] = (silu * up).astype(BF16)
            dg[:, cut] = (dhid * up * sig * (1.0 + gate * (1.0 - sig))).astype(BF16)
            du[:, cut] = (dhid * silu).astype(BF16)
            return 0

        lax.fori_loop(0, tiles, hidden_step, 0)
        acc[...] = jnp.zeros_like(acc)

        def model_step(j, _):
            cut = pl.ds(pl.multiple_of(j * td, td), td)
            out = jnp.dot(hh[...], wd[:, cut], preferred_element_type=F32).astype(BF16).astype(F32)
            prod = z[here, cut].astype(F32) * out
            folded = prod[:, 0:128]
            for k in range(1, td // 128):
                folded = folded + prod[:, k * 128 : (k + 1) * 128]
            acc[...] += folded
            dn = lax.dot_general(dg[...], wg[cut, :], NT, preferred_element_type=F32)
            dn = dn + lax.dot_general(du[...], wu[cut, :], NT, preferred_element_type=F32)
            wb[here, cut] = (weight * dn.astype(BF16).astype(F32)).astype(BF16)
            return 0

        lax.fori_loop(0, width // td, model_step, 0)
        dots = jnp.sum(acc[...], axis=1, keepdims=True).astype(BF16).astype(F32)
        for h in range(2):
            row = to_row(dots[h * rows : (h + 1) * rows, :])
            at[2 * g + h] = jnp.broadcast_to(row, (8, rows))

    def forward(g, between=None):
        normalize(fx, g)
        weight = route_weights(g, 1)
        here = pl.ds(2 * g * rows, 2 * rows)

        def hidden_step(j, _):
            cut = pl.ds(pl.multiple_of(j * tn, tn), tn)
            gate = jnp.dot(nrm[...], wg[:, cut], preferred_element_type=F32)
            up = jnp.dot(nrm[...], wu[:, cut], preferred_element_type=F32)
            hh[:, cut] = (gate * jax.nn.sigmoid(gate) * up).astype(BF16)
            if between is not None:
                between(j)
            return 0

        lax.fori_loop(0, tiles, hidden_step, 0)

        def model_step(j, _):
            cut = pl.ds(pl.multiple_of(j * td, td), td)
            out = jnp.dot(hh[...], wd[:, cut], preferred_element_type=F32).astype(BF16).astype(F32)
            wf[here, cut] = (weight * out).astype(BF16)
            return 0

        lax.fori_loop(0, width // td, model_step, 0)

    def chip_sums(i):
        keep, got = ((wb, rcb), (wf, rcf))[i]
        sums_to_core(i, 0).wait_recv()

        def step(q, _):
            keep[part(q), :] = (keep[part(q), :].astype(F32) + got[part(q), :].astype(F32)).astype(BF16)
            sums_to_link(i, q).start()
            return 0

        lax.fori_loop(0, n_chunks, step, 0)

    load_x(0).wait()
    load_x(1).wait()
    own_to_core(0).wait_recv()
    own_to_core(1).wait_recv()
    for s in (1, 2, 3):
        routes_to(s, 0).wait_recv()
        routes_to(s, 1).wait_recv()
    backward(0, True)
    sums_to_core(0, 0).start()
    dots_to(2).start()
    dots_to(3).start()
    load_x(2).wait()
    own_to_core(2).wait_recv()
    own_to_link(0).wait_recv()
    pass_to_core(0).start()
    forward(0)
    sums_to_core(1, 0).start()
    chip_sums(0)
    own_to_link(1).wait_recv()
    pass_to_core(1).start()
    chip_sums(1)

    pass_to_core(0).wait_recv()
    pass_to_core(1).wait_recv()
    backward(1, False)
    sums_to_core(0, 1).start()
    dots_to(1).start()
    own_to_link(2).wait_recv()
    pass_to_core(2).start()
    for s in (1, 2, 3):
        dots_to(s).wait_recv()
    tile = rts[0, 2].astype(F32)
    r0, r1 = to_col(tile[0:1, :]), to_col(tile[1:2, :])
    saved = cols[...]
    q0, q1 = saved[:, 0:1], saved[:, 1:2]
    total = q0 + q1
    a0, a1 = jnp.zeros((rows, 1), F32), jnp.zeros((rows, 1), F32)
    for s, owner in enumerate((e, e_c, e_l, e_d)):
        got = at[2] if s == 0 else ar[s]
        dot_col = to_col(got[0:1, :])
        a0 = a0 + jnp.where(r0 == owner.astype(F32), dot_col, 0.0)
        a1 = a1 + jnp.where(r1 == owner.astype(F32), dot_col, 0.0)
    mixed = a0 * (q0 / total) + a1 * (q1 / total)
    l0 = (a0 - mixed) / total * q0 * (1.0 - q0)
    l1 = (a1 - mixed) / total * q1 * (1.0 - q1)
    lane = lax.broadcasted_iota(jnp.int32, (rows, 128), 1).astype(F32)
    cols[...] = jnp.where(lane == r0, l0, 0.0) + jnp.where(lane == r1, l1, 0.0)
    sums_to_core(0, 1).wait_recv()

    def finish_backward(q, _):
        sums_to_link(0, q).wait_recv()
        for k in range(CHUNK // STEP):
            at_rows = pl.ds(pl.multiple_of(q * CHUNK + k * STEP, STEP), STEP)
            far = pl.ds(pl.multiple_of(2 * rows + q * CHUNK + k * STEP, STEP), STEP)
            near = pl.ds(pl.multiple_of(rows + q * CHUNK + k * STEP, STEP), STEP)
            wide = sx[far, :].astype(F32)
            inv = lax.rsqrt(jnp.mean(wide * wide, axis=1, keepdims=True) + EPSILON)
            dn = wb[far, :].astype(F32) + rcb[near, :].astype(F32) + lpb[at_rows, :].astype(F32)
            lcol = cols[at_rows, :]
            for j in range(4):
                dn = dn + lcol[:, j : j + 1] * rout[j : j + 1, :].astype(F32)
            scaled = dn * gain[...]
            mean = jnp.mean(scaled * wide, axis=1, keepdims=True)
            grad = z[far, :].astype(F32) + (inv * scaled - wide * (inv * inv * inv * mean))
            wb[far, :] = grad.astype(BF16)

        @pl.when(c > 0)
        def _():
            result(0, q).start()

        return 0

    early = n_chunks - tiles - 2
    lax.fori_loop(0, early, finish_backward, 0)
    pass_to_core(2).wait_recv()
    forward(1, lambda j: finish_backward(early + j, 0))
    sums_to_core(1, 1).start()
    lax.fori_loop(early + tiles, n_chunks, finish_backward, 0)
    nrm[0:rows, :] = jnp.zeros((rows, width), BF16)

    @pl.when(c == 0)
    def _():
        pltpu.make_async_copy(nrm.at[0:rows], fo_hbm, zero_sem.at[0]).start()

    @pl.when(c == n_pipe - 1)
    def _():
        pltpu.make_async_copy(nrm.at[0:rows], go_hbm, zero_sem.at[1]).start()

    sums_to_core(1, 1).wait_recv()

    def finish_forward(q, _):
        sums_to_link(1, q).wait_recv()
        for k in range(CHUNK // STEP):
            at_rows = pl.ds(pl.multiple_of(q * CHUNK + k * STEP, STEP), STEP)
            far = pl.ds(pl.multiple_of(2 * rows + q * CHUNK + k * STEP, STEP), STEP)
            near = pl.ds(pl.multiple_of(rows + q * CHUNK + k * STEP, STEP), STEP)
            out = wf[far, :].astype(F32) + rcf[near, :].astype(F32) + lpf[at_rows, :].astype(F32)
            wf[far, :] = (fx[far, :].astype(F32) + out).astype(BF16)

        @pl.when(c < n_pipe - 1)
        def _():
            result(1, q).start()

        return 0

    lax.fori_loop(0, n_chunks, finish_forward, 0)

    for s in (1, 2, 3):
        routes_to(s, 0).wait_send()
        routes_to(s, 1).wait_send()
        dots_to(s).wait_send()
    for i in range(3):
        own_to_core(i).wait_send()
        own_to_link(i).wait_send()
        pass_to_core(i).wait_send()
    for i in range(2):
        for g in range(2):
            sums_to_core(i, g).wait_send()
        for q in range(n_chunks):
            sums_to_link(i, q).wait_send()

    @pl.when(c > 0)
    def _():
        for q in range(n_chunks):
            result(0, q).wait_send()
            result(1, q).wait_recv()

    @pl.when(c < n_pipe - 1)
    def _():
        for q in range(n_chunks):
            result(1, q).wait_send()
            result(0, q).wait_recv()

    @pl.when(c == 0)
    def _():
        pltpu.make_async_copy(nrm.at[0:rows], fo_hbm, zero_sem.at[0]).wait()

    @pl.when(c == n_pipe - 1)
    def _():
        pltpu.make_async_copy(nrm.at[0:rows], go_hbm, zero_sem.at[1]).wait()


def settle(f_in, g_in, f_out, g_out, held, in_sem, out_sem):
    rows = f_in.shape[0]
    size = rows // 2
    moves = []
    for i, (src, dst) in enumerate(((f_in, f_out), (g_in, g_out))):
        for k in range(2):
            cut = pl.ds(k * size, size)
            moves.append((
                pltpu.make_async_copy(src.at[cut], held.at[i, cut], in_sem.at[i, k]),
                pltpu.make_async_copy(held.at[i, cut], dst.at[cut], out_sem.at[i, k]),
            ))
    for load, _ in moves:
        load.start()
    for load, store in moves:
        load.wait()
        store.start()
    for _, store in moves:
        store.wait()


def local(
    n_pipe, fwd_in, fwd_routes, saved_in, saved_routes, grad_in, norm_gain, router, w_gate, w_up, w_down
):
    rows, width = fwd_in.shape
    hidden = w_gate.shape[3]
    tn = min(256, hidden)
    td = 512 if width % 512 == 0 else 128
    n_chunks = rows // CHUNK
    dma = pltpu.SemaphoreType.DMA
    vmem = pl.BlockSpec(memory_space=pltpu.VMEM)
    hbm = pl.BlockSpec(memory_space=pl.ANY)
    grad_out_type = jax.ShapeDtypeStruct((rows, width), BF16)
    fwd_out, grad_out = pl.pallas_call(
        functools.partial(kernel, n_pipe, tn, td),
        out_shape=(grad_out_type, grad_out_type),
        in_specs=[hbm, hbm, hbm, vmem, vmem, vmem, vmem, hbm, hbm, hbm],
        out_specs=(hbm, hbm),
        scratch_shapes=[
            pltpu.VMEM((4 * rows, width), BF16),
            pltpu.VMEM((4 * rows, width), BF16),
            pltpu.VMEM((4 * rows, width), BF16),
            pltpu.VMEM((2, 4, 2, rows), jnp.int32),
            pltpu.VMEM((width, hidden), BF16),
            pltpu.VMEM((width, hidden), BF16),
            pltpu.VMEM((hidden, width), BF16),
            pltpu.VMEM((128, width), BF16),
            pltpu.VMEM((2 * rows, width), BF16),
            pltpu.VMEM((2 * rows, hidden), BF16),
            pltpu.VMEM((2 * rows, hidden), BF16),
            pltpu.VMEM((2 * rows, hidden), BF16),
            pltpu.VMEM((2 * rows, 128), F32),
            pltpu.VMEM((rows, 128), F32),
            pltpu.VMEM((4 * rows, width), BF16),
            pltpu.VMEM((4 * rows, width), BF16),
            pltpu.VMEM((2 * rows, width), BF16),
            pltpu.VMEM((2 * rows, width), BF16),
            pltpu.VMEM((rows, width), BF16),
            pltpu.VMEM((rows, width), BF16),
            pltpu.VMEM((4, 8, rows), F32),
            pltpu.VMEM((4, 8, rows), F32),
            dma((3,)), dma((3, hidden // tn)),
            dma((10,)), dma((10,)),
            dma((3,)), dma((3,)),
            dma((6,)), dma((6,)),
            dma((3,)), dma((3,)),
            dma((n_chunks,)), dma((n_chunks,)),
            dma((n_chunks,)), dma((n_chunks,)),
            dma((n_chunks,)), dma((n_chunks,)),
            dma((n_chunks,)), dma((n_chunks,)),
            dma((2,)),
        ],
        compiler_params=pltpu.CompilerParams(
            collective_id=0, has_side_effects=True, vmem_limit_bytes=67043328
        ),
        name="relay_slot",
    )(saved_in, grad_in, fwd_in, saved_routes.T, fwd_routes.T, norm_gain, router[0].T, w_gate, w_up, w_down)
    return pl.pallas_call(
        settle,
        out_shape=(grad_out_type, grad_out_type),
        in_specs=[hbm, hbm],
        out_specs=(hbm, hbm),
        scratch_shapes=[pltpu.VMEM((2, rows, width), BF16), dma((2, 2)), dma((2, 2))],
        name="settle",
    )(fwd_out, grad_out)


def solution(mesh):
    rows = P(("pipe", "expert"), None)
    in_specs = (
        rows, rows, rows, rows, rows,
        P("pipe", None),
        P("pipe", None, None),
        P("pipe", "expert", None, None),
        P("pipe", "expert", None, None),
        P("pipe", "expert", None, None),
    )
    return jax.shard_map(
        functools.partial(local, mesh.shape["pipe"]),
        mesh=mesh, in_specs=in_specs, out_specs=(rows, rows), check_vma=False,
    )
```

```python
import functools

import jax
import jax.numpy as jnp
from jax import lax
from jax.experimental import pallas as pl
from jax.experimental.pallas import tpu as pltpu
from jax.sharding import PartitionSpec as P

EPSILON = 1e-06
MESH = pl.DeviceIdType.MESH
F32 = jnp.float32
BF16 = jnp.bfloat16
NT = (((1,), (1,)), ((), ()))
CHUNK = 16
FINE = 16
STEP = 16


def kernel(
    n_pipe, tn, td,
    sx_hbm, z_hbm, fx_hbm, rt_s, rt_f, gain, rout, wg_hbm, wu_hbm, wd_hbm,
    fo_hbm, go_hbm,
    sx, z, fx, rts, wg, wu, wd, rb, nrm, hh, dg, du, acc, cols, wb, wf, rcb, rcf, lpb, lpf, at, ar,
    loc_sem, w_sem, c_send, c_recv, l_send, l_recv, r_send, r_recv, t_send, t_recv, pb_send, pb_recv, pf_send, pf_recv,
    go_send, go_recv, fo_send, fo_recv, zero_sem,
):
    c = lax.axis_index("pipe")
    e = lax.axis_index("expert")
    rows, width = sx_hbm.shape
    hidden = hh.shape[1]
    e_c = e + 1 - 2 * lax.rem(e, 2)
    e_l = lax.rem(e + 2, 4)
    e_d = lax.rem(e_c + 2, 4)
    core, link, diag = (c, e_c), (c, e_l), (c, e_d)
    after, before = (c + 1, e_l), (c - 1, e_l)
    n_chunks = rows // CHUNK

    def block(s):
        return pl.ds(s * rows, rows)

    def remote(src, dst, send, recv, to):
        return pltpu.make_async_remote_copy(
            src_ref=src, dst_ref=dst, send_sem=send, recv_sem=recv, device_id=to, device_id_type=MESH
        )

    def load_x(i):
        src, dst = ((sx_hbm, sx), (z_hbm, z), (fx_hbm, fx))[i]
        return pltpu.make_async_copy(src, dst.at[block(0)], loc_sem.at[i])

    def load_w(i, j):
        part = pl.ds(pl.multiple_of(j * tn, tn), tn)
        if i == 2:
            return pltpu.make_async_copy(wd_hbm.at[0, 0, part], wd.at[part], w_sem.at[i, j])
        src, dst = ((wg_hbm, wg), (wu_hbm, wu))[i]
        return pltpu.make_async_copy(src.at[0, 0, :, part], dst.at[:, part], w_sem.at[i, j])

    def own_to_core(i):
        src, dst = ((sx_hbm, sx), (z_hbm, z), (fx_hbm, fx))[i]
        return remote(src, dst.at[block(1)], c_send.at[i], c_recv.at[i], core)

    def own_to_link(i):
        src, dst = ((sx_hbm, sx), (z_hbm, z), (fx_hbm, fx))[i]
        return remote(src, dst.at[block(2)], l_send.at[i], l_recv.at[i], link)

    def pass_to_core(i):
        ref = (sx, z, fx)[i]
        return remote(ref.at[block(2)], ref.at[block(3)], c_send.at[3 + i], c_recv.at[3 + i], core)

    def sums_to_core(i, g):
        src, dst = ((wb, rcb), (wf, rcf))[i]
        k = 6 + 2 * i + g
        return remote(src.at[block(2 * g + 1)], dst.at[block(g)], c_send.at[k], c_recv.at[k], core)

    def routes_to(s, kind):
        k = 3 * kind + s - 1
        return remote((rt_s, rt_f)[kind], rts.at[kind, s], r_send.at[k], r_recv.at[k], (core, link, diag)[s - 1])

    def dots_to(s):
        t = (None, 3, 0, 1)[s]
        return remote(at.at[t], ar.at[s], t_send.at[s - 1], t_recv.at[s - 1], (core, link, diag)[s - 1])

    sizes = (CHUNK, FINE)
    counts = (rows // CHUNK, rows // FINE)

    def part(i, q):
        return pl.ds(pl.multiple_of(q * sizes[i], sizes[i]), sizes[i])

    def tail(i, q):
        return pl.ds(pl.multiple_of(2 * rows + q * sizes[i], sizes[i]), sizes[i])

    def sums_to_link(i, q):
        src, dst, send, recv = ((wb, lpb, pb_send, pb_recv), (wf, lpf, pf_send, pf_recv))[i]
        return remote(src.at[part(i, q)], dst.at[part(i, q)], send.at[q], recv.at[q], link)

    def result(i, q):
        if i == 0:
            return remote(wb.at[tail(0, q)], go_hbm.at[part(0, q)], go_send.at[q], go_recv.at[q], before)
        return remote(wf.at[tail(1, q)], fo_hbm.at[part(1, q)], fo_send.at[q], fo_recv.at[q], after)

    tiles = hidden // tn
    load_x(0).start()
    for j in range(tiles):
        load_w(0, j).start()
        load_w(1, j).start()
        if j == 0:
            load_x(1).start()
        load_w(2, j).start()
    load_x(2).start()

    barrier = pltpu.get_barrier_semaphore()
    ring = [(lax.rem(c + by, n_pipe), e_l) for by in (1, n_pipe - 1)]
    for peer in (core, link, diag, *ring):
        pl.semaphore_signal(barrier, inc=1, device_id=peer, device_id_type=MESH)
    pl.semaphore_wait(barrier, 5)

    for s in (1, 2, 3):
        routes_to(s, 0).start()
        routes_to(s, 1).start()
    for i in range(3):
        own_to_link(i).start()
        own_to_core(i).start()

    rts[0, 0] = rt_s[...]
    rts[1, 0] = rt_f[...]
    rb[...] = jnp.zeros_like(rb)
    table = rout[...].astype(F32)
    rb[0:16, :] = jnp.concatenate([table, jnp.zeros((12, width), F32)], axis=0).astype(BF16)
    eye = lax.broadcasted_iota(jnp.int32, (rows, rows), 0) == lax.broadcasted_iota(jnp.int32, (rows, rows), 1)

    def to_col(row):
        return jnp.sum(jnp.where(eye, row, 0.0), axis=1, keepdims=True)

    def to_row(col):
        return jnp.sum(jnp.where(eye, col, 0.0), axis=0, keepdims=True)

    def normalize(x_ref, g):
        def step(q, _):
            at_rows = pl.ds(pl.multiple_of(2 * g * rows + q * STEP, STEP), STEP)
            to_rows = pl.ds(pl.multiple_of(q * STEP, STEP), STEP)
            wide = x_ref[at_rows, :].astype(F32)
            inv = lax.rsqrt(jnp.mean(wide * wide, axis=1, keepdims=True) + EPSILON)
            nrm[to_rows, :] = (wide * inv * gain[...]).astype(BF16)
            return 0

        lax.fori_loop(0, 2 * rows // STEP, step, 0)

    def route_weights(g, kind):
        logits = lax.dot_general(nrm[...], rb[...], NT, preferred_element_type=F32)
        scores = jax.nn.sigmoid(logits)
        lane = lax.broadcasted_iota(jnp.int32, (rows, 128), 1).astype(F32)
        me = e.astype(F32)
        out = []
        for h in range(2):
            s = 2 * g + h
            tile = rts[kind, s].astype(F32)
            r0, r1 = to_col(tile[0:1, :]), to_col(tile[1:2, :])
            mine = scores[h * rows : (h + 1) * rows, :]
            q0 = jnp.sum(jnp.where(lane == r0, mine, 0.0), axis=1, keepdims=True)
            q1 = jnp.sum(jnp.where(lane == r1, mine, 0.0), axis=1, keepdims=True)
            total = q0 + q1
            out.append(jnp.where(r0 == me, q0 / total, 0.0) + jnp.where(r1 == me, q1 / total, 0.0))
            if s == 2 and kind == 0:
                cols[...] = jnp.where(lane == 0.0, q0, jnp.where(lane == 1.0, q1, 0.0))
        return jnp.concatenate(out, axis=0)

    def backward(g, first):
        normalize(sx, g)
        weight = route_weights(g, 0)
        here = pl.ds(2 * g * rows, 2 * rows)

        def hidden_step(j, _):
            cut = pl.ds(pl.multiple_of(j * tn, tn), tn)
            if first:
                for i in range(3):
                    load_w(i, j).wait()
            gate = jnp.dot(nrm[...], wg[:, cut], preferred_element_type=F32)
            up = jnp.dot(nrm[...], wu[:, cut], preferred_element_type=F32)
            dhid = lax.dot_general(z[here, :], wd[cut, :], NT, preferred_element_type=F32)
            sig = jax.nn.sigmoid(gate)
            silu = gate * sig
            hh[:, cut] = (silu * up).astype(BF16)
            dg[:, cut] = (dhid * up * sig * (1.0 + gate * (1.0 - sig))).astype(BF16)
            du[:, cut] = (dhid * silu).astype(BF16)
            return 0

        lax.fori_loop(0, tiles, hidden_step, 0)
        acc[...] = jnp.zeros_like(acc)

        def model_step(j, _):
            cut = pl.ds(pl.multiple_of(j * td, td), td)
            out = jnp.dot(hh[...], wd[:, cut], preferred_element_type=F32).astype(BF16).astype(F32)
            prod = z[here, cut].astype(F32) * out
            folded = prod[:, 0:128]
            for k in range(1, td // 128):
                folded = folded + prod[:, k * 128 : (k + 1) * 128]
            acc[...] += folded
            dn = lax.dot_general(dg[...], wg[cut, :], NT, preferred_element_type=F32)
            dn = dn + lax.dot_general(du[...], wu[cut, :], NT, preferred_element_type=F32)
            wb[here, cut] = (weight * dn.astype(BF16).astype(F32)).astype(BF16)
            return 0

        lax.fori_loop(0, width // td, model_step, 0)
        dots = jnp.sum(acc[...], axis=1, keepdims=True).astype(BF16).astype(F32)
        for h in range(2):
            row = to_row(dots[h * rows : (h + 1) * rows, :])
            at[2 * g + h] = jnp.broadcast_to(row, (8, rows))

    def forward(g, between=None):
        normalize(fx, g)
        weight = route_weights(g, 1)
        here = pl.ds(2 * g * rows, 2 * rows)

        def hidden_step(j, _):
            cut = pl.ds(pl.multiple_of(j * tn, tn), tn)
            gate = jnp.dot(nrm[...], wg[:, cut], preferred_element_type=F32)
            up = jnp.dot(nrm[...], wu[:, cut], preferred_element_type=F32)
            hh[:, cut] = (gate * jax.nn.sigmoid(gate) * up).astype(BF16)
            if between is not None:
                between(j)
            return 0

        lax.fori_loop(0, tiles, hidden_step, 0)

        def model_step(j, _):
            cut = pl.ds(pl.multiple_of(j * td, td), td)
            out = jnp.dot(hh[...], wd[:, cut], preferred_element_type=F32).astype(BF16).astype(F32)
            wf[here, cut] = (weight * out).astype(BF16)
            return 0

        lax.fori_loop(0, width // td, model_step, 0)

    def chip_sums(i):
        keep, got = ((wb, rcb), (wf, rcf))[i]
        sums_to_core(i, 0).wait_recv()

        def step(q, _):
            cut = part(i, q)
            keep[cut, :] = (keep[cut, :].astype(F32) + got[cut, :].astype(F32)).astype(BF16)
            sums_to_link(i, q).start()
            return 0

        lax.fori_loop(0, counts[i], step, 0)

    load_x(0).wait()
    load_x(1).wait()
    own_to_core(0).wait_recv()
    own_to_core(1).wait_recv()
    for s in (1, 2, 3):
        routes_to(s, 0).wait_recv()
        routes_to(s, 1).wait_recv()
    backward(0, True)
    sums_to_core(0, 0).start()
    dots_to(2).start()
    dots_to(3).start()
    load_x(2).wait()
    own_to_core(2).wait_recv()
    own_to_link(0).wait_recv()
    pass_to_core(0).start()
    forward(0)
    sums_to_core(1, 0).start()
    chip_sums(0)
    own_to_link(1).wait_recv()
    pass_to_core(1).start()
    chip_sums(1)

    pass_to_core(0).wait_recv()
    pass_to_core(1).wait_recv()
    backward(1, False)
    sums_to_core(0, 1).start()
    dots_to(1).start()
    own_to_link(2).wait_recv()
    pass_to_core(2).start()
    for s in (1, 2, 3):
        dots_to(s).wait_recv()
    tile = rts[0, 2].astype(F32)
    r0, r1 = to_col(tile[0:1, :]), to_col(tile[1:2, :])
    saved = cols[...]
    q0, q1 = saved[:, 0:1], saved[:, 1:2]
    total = q0 + q1
    a0, a1 = jnp.zeros((rows, 1), F32), jnp.zeros((rows, 1), F32)
    for s, owner in enumerate((e, e_c, e_l, e_d)):
        got = at[2] if s == 0 else ar[s]
        dot_col = to_col(got[0:1, :])
        a0 = a0 + jnp.where(r0 == owner.astype(F32), dot_col, 0.0)
        a1 = a1 + jnp.where(r1 == owner.astype(F32), dot_col, 0.0)
    mixed = a0 * (q0 / total) + a1 * (q1 / total)
    l0 = (a0 - mixed) / total * q0 * (1.0 - q0)
    l1 = (a1 - mixed) / total * q1 * (1.0 - q1)
    lane = lax.broadcasted_iota(jnp.int32, (rows, 128), 1).astype(F32)
    cols[...] = jnp.where(lane == r0, l0, 0.0) + jnp.where(lane == r1, l1, 0.0)
    sums_to_core(0, 1).wait_recv()

    def finish_backward(q, _):
        sums_to_link(0, q).wait_recv()
        for k in range(CHUNK // STEP):
            at_rows = pl.ds(pl.multiple_of(q * CHUNK + k * STEP, STEP), STEP)
            far = pl.ds(pl.multiple_of(2 * rows + q * CHUNK + k * STEP, STEP), STEP)
            near = pl.ds(pl.multiple_of(rows + q * CHUNK + k * STEP, STEP), STEP)
            wide = sx[far, :].astype(F32)
            inv = lax.rsqrt(jnp.mean(wide * wide, axis=1, keepdims=True) + EPSILON)
            dn = wb[far, :].astype(F32) + rcb[near, :].astype(F32) + lpb[at_rows, :].astype(F32)
            lcol = cols[at_rows, :]
            for j in range(4):
                dn = dn + lcol[:, j : j + 1] * rout[j : j + 1, :].astype(F32)
            scaled = dn * gain[...]
            mean = jnp.mean(scaled * wide, axis=1, keepdims=True)
            grad = z[far, :].astype(F32) + (inv * scaled - wide * (inv * inv * inv * mean))
            wb[far, :] = grad.astype(BF16)

        @pl.when(c > 0)
        def _():
            result(0, q).start()

        return 0

    early = n_chunks - tiles - 2
    lax.fori_loop(0, early, finish_backward, 0)
    pass_to_core(2).wait_recv()
    forward(1, lambda j: finish_backward(early + j, 0))
    sums_to_core(1, 1).start()
    lax.fori_loop(early + tiles, n_chunks, finish_backward, 0)
    nrm[0:rows, :] = jnp.zeros((rows, width), BF16)

    @pl.when(c == 0)
    def _():
        pltpu.make_async_copy(nrm.at[0:rows], fo_hbm, zero_sem.at[0]).start()

    @pl.when(c == n_pipe - 1)
    def _():
        pltpu.make_async_copy(nrm.at[0:rows], go_hbm, zero_sem.at[1]).start()

    sums_to_core(1, 1).wait_recv()

    def finish_forward(q, _):
        sums_to_link(1, q).wait_recv()
        far = tail(1, q)
        near = pl.ds(pl.multiple_of(rows + q * FINE, FINE), FINE)
        out = wf[far, :].astype(F32) + rcf[near, :].astype(F32) + lpf[part(1, q), :].astype(F32)
        wf[far, :] = (fx[far, :].astype(F32) + out).astype(BF16)

        @pl.when(c < n_pipe - 1)
        def _():
            result(1, q).start()

        return 0

    lax.fori_loop(0, counts[1], finish_forward, 0)

    for s in (1, 2, 3):
        routes_to(s, 0).wait_send()
        routes_to(s, 1).wait_send()
        dots_to(s).wait_send()
    for i in range(3):
        own_to_core(i).wait_send()
        own_to_link(i).wait_send()
        pass_to_core(i).wait_send()
    for i in range(2):
        for g in range(2):
            sums_to_core(i, g).wait_send()
        for q in range(counts[i]):
            sums_to_link(i, q).wait_send()

    @pl.when(c > 0)
    def _():
        for q in range(counts[0]):
            result(0, q).wait_send()
        for q in range(counts[1]):
            result(1, q).wait_recv()

    @pl.when(c < n_pipe - 1)
    def _():
        for q in range(counts[1]):
            result(1, q).wait_send()
        for q in range(counts[0]):
            result(0, q).wait_recv()

    @pl.when(c == 0)
    def _():
        pltpu.make_async_copy(nrm.at[0:rows], fo_hbm, zero_sem.at[0]).wait()

    @pl.when(c == n_pipe - 1)
    def _():
        pltpu.make_async_copy(nrm.at[0:rows], go_hbm, zero_sem.at[1]).wait()


def local(
    n_pipe, fwd_in, fwd_routes, saved_in, saved_routes, grad_in, norm_gain, router, w_gate, w_up, w_down
):
    rows, width = fwd_in.shape
    hidden = w_gate.shape[3]
    tn = min(256, hidden)
    td = 512 if width % 512 == 0 else 128
    n_chunks = rows // CHUNK
    dma = pltpu.SemaphoreType.DMA
    vmem = pl.BlockSpec(memory_space=pltpu.VMEM)
    hbm = pl.BlockSpec(memory_space=pl.ANY)
    grad_out_type = jax.ShapeDtypeStruct((rows, width), BF16)
    held_type = pltpu.VMEM((rows, width), BF16)
    fwd_out, grad_out = pl.pallas_call(
        functools.partial(kernel, n_pipe, tn, td),
        out_shape=(held_type, held_type),
        in_specs=[hbm, hbm, hbm, vmem, vmem, vmem, vmem, hbm, hbm, hbm],
        out_specs=(vmem, vmem),
        scratch_shapes=[
            pltpu.VMEM((4 * rows, width), BF16),
            pltpu.VMEM((4 * rows, width), BF16),
            pltpu.VMEM((4 * rows, width), BF16),
            pltpu.VMEM((2, 4, 2, rows), jnp.int32),
            pltpu.VMEM((width, hidden), BF16),
            pltpu.VMEM((width, hidden), BF16),
            pltpu.VMEM((hidden, width), BF16),
            pltpu.VMEM((128, width), BF16),
            pltpu.VMEM((2 * rows, width), BF16),
            pltpu.VMEM((2 * rows, hidden), BF16),
            pltpu.VMEM((2 * rows, hidden), BF16),
            pltpu.VMEM((2 * rows, hidden), BF16),
            pltpu.VMEM((2 * rows, 128), F32),
            pltpu.VMEM((rows, 128), F32),
            pltpu.VMEM((4 * rows, width), BF16),
            pltpu.VMEM((4 * rows, width), BF16),
            pltpu.VMEM((2 * rows, width), BF16),
            pltpu.VMEM((2 * rows, width), BF16),
            pltpu.VMEM((rows, width), BF16),
            pltpu.VMEM((rows, width), BF16),
            pltpu.VMEM((4, 8, rows), F32),
            pltpu.VMEM((4, 8, rows), F32),
            dma((3,)), dma((3, hidden // tn)),
            dma((10,)), dma((10,)),
            dma((3,)), dma((3,)),
            dma((6,)), dma((6,)),
            dma((3,)), dma((3,)),
            dma((n_chunks,)), dma((n_chunks,)),
            dma((rows // FINE,)), dma((rows // FINE,)),
            dma((n_chunks,)), dma((n_chunks,)),
            dma((rows // FINE,)), dma((rows // FINE,)),
            dma((2,)),
        ],
        compiler_params=pltpu.CompilerParams(
            collective_id=0, has_side_effects=True, vmem_limit_bytes=60 * 1024 * 1024
        ),
        name="relay_slot",
    )(saved_in, grad_in, fwd_in, saved_routes.T, fwd_routes.T, norm_gain, router[0].T, w_gate, w_up, w_down)
    return fwd_out, grad_out


def solution(mesh):
    rows = P(("pipe", "expert"), None)
    in_specs = (
        rows, rows, rows, rows, rows,
        P("pipe", None),
        P("pipe", None, None),
        P("pipe", "expert", None, None),
        P("pipe", "expert", None, None),
        P("pipe", "expert", None, None),
    )
    return jax.shard_map(
        functools.partial(local, mesh.shape["pipe"]),
        mesh=mesh, in_specs=in_specs, out_specs=(rows, rows), check_vma=False,
    )
```

```python
import functools

import jax
import jax.numpy as jnp
from jax import lax
from jax.experimental import pallas as pl
from jax.experimental.pallas import tpu as pltpu
from jax.sharding import PartitionSpec as P

EPSILON = 1e-06
MESH = pl.DeviceIdType.MESH
F32 = jnp.float32
BF16 = jnp.bfloat16
NT = (((1,), (1,)), ((), ()))
CHUNK = 16
FINE = 16
STEP = 16


def kernel(
    n_pipe, tn, td,
    sx_hbm, z_hbm, fx_hbm, rt_s, rt_f, gain, rout, wg_hbm, wu_hbm, wd_hbm,
    fo_hbm, go_hbm,
    sx, z, fx, rts, wg, wu, wd, rb, nrm, hh, dg, du, acc, cols, wb, wf, rcb, rcf, lpb, lpf, at, ar,
    loc_sem, w_sem, c_send, c_recv, l_send, l_recv, r_send, r_recv, t_send, t_recv, pb_send, pb_recv, pf_send, pf_recv,
    go_send, go_recv, fo_send, fo_recv, zero_sem,
):
    c = lax.axis_index("pipe")
    e = lax.axis_index("expert")
    rows, width = sx_hbm.shape
    hidden = hh.shape[1]
    e_c = e + 1 - 2 * lax.rem(e, 2)
    e_l = lax.rem(e + 2, 4)
    e_d = lax.rem(e_c + 2, 4)
    core, link, diag = (c, e_c), (c, e_l), (c, e_d)
    after, before = (c + 1, e_l), (c - 1, e_l)
    n_chunks = rows // CHUNK

    def block(s):
        return pl.ds(s * rows, rows)

    def remote(src, dst, send, recv, to):
        return pltpu.make_async_remote_copy(
            src_ref=src, dst_ref=dst, send_sem=send, recv_sem=recv, device_id=to, device_id_type=MESH
        )

    def load_x(i):
        src, dst = ((sx_hbm, sx), (z_hbm, z), (fx_hbm, fx))[i]
        return pltpu.make_async_copy(src, dst.at[block(0)], loc_sem.at[i])

    def load_w(i, j):
        part = pl.ds(pl.multiple_of(j * tn, tn), tn)
        if i == 2:
            return pltpu.make_async_copy(wd_hbm.at[0, 0, part], wd.at[part], w_sem.at[i, j])
        src, dst = ((wg_hbm, wg), (wu_hbm, wu))[i]
        return pltpu.make_async_copy(src.at[0, 0, :, part], dst.at[:, part], w_sem.at[i, j])

    def own_to_core(i):
        src, dst = ((sx_hbm, sx), (z_hbm, z), (fx_hbm, fx))[i]
        return remote(src, dst.at[block(1)], c_send.at[i], c_recv.at[i], core)

    def own_to_link(i):
        src, dst = ((sx_hbm, sx), (z_hbm, z), (fx_hbm, fx))[i]
        return remote(src, dst.at[block(2)], l_send.at[i], l_recv.at[i], link)

    def pass_to_core(i):
        ref = (sx, z, fx)[i]
        return remote(ref.at[block(2)], ref.at[block(3)], c_send.at[3 + i], c_recv.at[3 + i], core)

    def sums_to_core(i, g):
        src, dst = ((wb, rcb), (wf, rcf))[i]
        k = 6 + 2 * i + g
        return remote(src.at[block(2 * g + 1)], dst.at[block(g)], c_send.at[k], c_recv.at[k], core)

    def routes_to(s, kind):
        k = 3 * kind + s - 1
        return remote((rt_s, rt_f)[kind], rts.at[kind, s], r_send.at[k], r_recv.at[k], (core, link, diag)[s - 1])

    def dots_to(s):
        t = (None, 3, 0, 1)[s]
        return remote(at.at[t], ar.at[s], t_send.at[s - 1], t_recv.at[s - 1], (core, link, diag)[s - 1])

    sizes = (CHUNK, FINE)
    counts = (rows // CHUNK, rows // FINE)

    def part(i, q):
        return pl.ds(pl.multiple_of(q * sizes[i], sizes[i]), sizes[i])

    def tail(i, q):
        return pl.ds(pl.multiple_of(2 * rows + q * sizes[i], sizes[i]), sizes[i])

    def sums_to_link(i, q):
        src, dst, send, recv = ((wb, lpb, pb_send, pb_recv), (wf, lpf, pf_send, pf_recv))[i]
        return remote(src.at[part(i, q)], dst.at[part(i, q)], send.at[q], recv.at[q], link)

    def result(i, q):
        if i == 0:
            return remote(wb.at[tail(0, q)], go_hbm.at[part(0, q)], go_send.at[q], go_recv.at[q], before)
        return remote(wf.at[tail(1, q)], fo_hbm.at[part(1, q)], fo_send.at[q], fo_recv.at[q], after)

    tiles = hidden // tn
    barrier = pltpu.get_barrier_semaphore()
    ring = [(lax.rem(c + by, n_pipe), e_l) for by in (1, n_pipe - 1)]
    for peer in (core, link, diag, *ring):
        pl.semaphore_signal(barrier, inc=1, device_id=peer, device_id_type=MESH)
    load_x(0).start()
    for j in range(tiles):
        load_w(0, j).start()
        load_w(1, j).start()
        if j == 0:
            load_x(1).start()
        load_w(2, j).start()
    load_x(2).start()
    pl.semaphore_wait(barrier, 5)

    for s in (1, 2, 3):
        routes_to(s, 0).start()
        routes_to(s, 1).start()
    for i in range(3):
        own_to_link(i).start()
        own_to_core(i).start()

    rts[0, 0] = rt_s[...]
    rts[1, 0] = rt_f[...]
    rb[...] = jnp.zeros_like(rb)
    table = rout[...].astype(F32)
    rb[0:16, :] = jnp.concatenate([table, jnp.zeros((12, width), F32)], axis=0).astype(BF16)
    eye = lax.broadcasted_iota(jnp.int32, (rows, rows), 0) == lax.broadcasted_iota(jnp.int32, (rows, rows), 1)

    def to_col(row):
        return jnp.sum(jnp.where(eye, row, 0.0), axis=1, keepdims=True)

    def to_row(col):
        return jnp.sum(jnp.where(eye, col, 0.0), axis=0, keepdims=True)

    def normalize(x_ref, g):
        def step(q, _):
            at_rows = pl.ds(pl.multiple_of(2 * g * rows + q * STEP, STEP), STEP)
            to_rows = pl.ds(pl.multiple_of(q * STEP, STEP), STEP)
            wide = x_ref[at_rows, :].astype(F32)
            inv = lax.rsqrt(jnp.mean(wide * wide, axis=1, keepdims=True) + EPSILON)
            nrm[to_rows, :] = (wide * inv * gain[...]).astype(BF16)
            return 0

        lax.fori_loop(0, 2 * rows // STEP, step, 0)

    def route_weights(g, kind):
        logits = lax.dot_general(nrm[...], rb[...], NT, preferred_element_type=F32)
        scores = jax.nn.sigmoid(logits)
        lane = lax.broadcasted_iota(jnp.int32, (rows, 128), 1).astype(F32)
        me = e.astype(F32)
        out = []
        for h in range(2):
            s = 2 * g + h
            tile = rts[kind, s].astype(F32)
            r0, r1 = to_col(tile[0:1, :]), to_col(tile[1:2, :])
            mine = scores[h * rows : (h + 1) * rows, :]
            q0 = jnp.sum(jnp.where(lane == r0, mine, 0.0), axis=1, keepdims=True)
            q1 = jnp.sum(jnp.where(lane == r1, mine, 0.0), axis=1, keepdims=True)
            total = q0 + q1
            out.append(jnp.where(r0 == me, q0 / total, 0.0) + jnp.where(r1 == me, q1 / total, 0.0))
            if s == 2 and kind == 0:
                cols[...] = jnp.where(lane == 0.0, q0, jnp.where(lane == 1.0, q1, 0.0))
        return jnp.concatenate(out, axis=0)

    def backward(g, first):
        normalize(sx, g)
        weight = route_weights(g, 0)
        here = pl.ds(2 * g * rows, 2 * rows)

        def hidden_step(j, _):
            cut = pl.ds(pl.multiple_of(j * tn, tn), tn)
            if first:
                for i in range(3):
                    load_w(i, j).wait()
            gate = jnp.dot(nrm[...], wg[:, cut], preferred_element_type=F32)
            up = jnp.dot(nrm[...], wu[:, cut], preferred_element_type=F32)
            dhid = lax.dot_general(z[here, :], wd[cut, :], NT, preferred_element_type=F32)
            sig = jax.nn.sigmoid(gate)
            silu = gate * sig
            hh[:, cut] = (silu * up).astype(BF16)
            dg[:, cut] = (dhid * up * sig * (1.0 + gate * (1.0 - sig))).astype(BF16)
            du[:, cut] = (dhid * silu).astype(BF16)
            return 0

        lax.fori_loop(0, tiles, hidden_step, 0)
        acc[...] = jnp.zeros_like(acc)

        def model_step(j, _):
            cut = pl.ds(pl.multiple_of(j * td, td), td)
            out = jnp.dot(hh[...], wd[:, cut], preferred_element_type=F32).astype(BF16).astype(F32)
            prod = z[here, cut].astype(F32) * out
            folded = prod[:, 0:128]
            for k in range(1, td // 128):
                folded = folded + prod[:, k * 128 : (k + 1) * 128]
            acc[...] += folded
            dn = lax.dot_general(dg[...], wg[cut, :], NT, preferred_element_type=F32)
            dn = dn + lax.dot_general(du[...], wu[cut, :], NT, preferred_element_type=F32)
            wb[here, cut] = (weight * dn.astype(BF16).astype(F32)).astype(BF16)
            return 0

        lax.fori_loop(0, width // td, model_step, 0)
        dots = jnp.sum(acc[...], axis=1, keepdims=True).astype(BF16).astype(F32)
        for h in range(2):
            row = to_row(dots[h * rows : (h + 1) * rows, :])
            at[2 * g + h] = jnp.broadcast_to(row, (8, rows))

    def forward(g, between=None):
        normalize(fx, g)
        weight = route_weights(g, 1)
        here = pl.ds(2 * g * rows, 2 * rows)

        def hidden_step(j, _):
            cut = pl.ds(pl.multiple_of(j * tn, tn), tn)
            gate = jnp.dot(nrm[...], wg[:, cut], preferred_element_type=F32)
            up = jnp.dot(nrm[...], wu[:, cut], preferred_element_type=F32)
            hh[:, cut] = (gate * jax.nn.sigmoid(gate) * up).astype(BF16)
            if between is not None:
                between(j)
            return 0

        lax.fori_loop(0, tiles, hidden_step, 0)

        def model_step(j, _):
            cut = pl.ds(pl.multiple_of(j * td, td), td)
            out = jnp.dot(hh[...], wd[:, cut], preferred_element_type=F32).astype(BF16).astype(F32)
            wf[here, cut] = (weight * out).astype(BF16)
            return 0

        lax.fori_loop(0, width // td, model_step, 0)

    def chip_sums(i):
        keep, got = ((wb, rcb), (wf, rcf))[i]
        sums_to_core(i, 0).wait_recv()

        def step(q, _):
            cut = part(i, q)
            keep[cut, :] = (keep[cut, :].astype(F32) + got[cut, :].astype(F32)).astype(BF16)
            sums_to_link(i, q).start()
            return 0

        lax.fori_loop(0, counts[i], step, 0)

    load_x(0).wait()
    load_x(1).wait()
    own_to_core(0).wait_recv()
    own_to_core(1).wait_recv()
    for s in (1, 2, 3):
        routes_to(s, 0).wait_recv()
        routes_to(s, 1).wait_recv()
    backward(0, True)
    sums_to_core(0, 0).start()
    dots_to(2).start()
    dots_to(3).start()
    load_x(2).wait()
    own_to_core(2).wait_recv()
    own_to_link(0).wait_recv()
    pass_to_core(0).start()
    forward(0)
    sums_to_core(1, 0).start()
    chip_sums(0)
    own_to_link(1).wait_recv()
    pass_to_core(1).start()
    chip_sums(1)

    pass_to_core(0).wait_recv()
    pass_to_core(1).wait_recv()
    backward(1, False)
    sums_to_core(0, 1).start()
    dots_to(1).start()
    own_to_link(2).wait_recv()
    pass_to_core(2).start()
    for s in (1, 2, 3):
        dots_to(s).wait_recv()
    tile = rts[0, 2].astype(F32)
    r0, r1 = to_col(tile[0:1, :]), to_col(tile[1:2, :])
    saved = cols[...]
    q0, q1 = saved[:, 0:1], saved[:, 1:2]
    total = q0 + q1
    a0, a1 = jnp.zeros((rows, 1), F32), jnp.zeros((rows, 1), F32)
    for s, owner in enumerate((e, e_c, e_l, e_d)):
        got = at[2] if s == 0 else ar[s]
        dot_col = to_col(got[0:1, :])
        a0 = a0 + jnp.where(r0 == owner.astype(F32), dot_col, 0.0)
        a1 = a1 + jnp.where(r1 == owner.astype(F32), dot_col, 0.0)
    mixed = a0 * (q0 / total) + a1 * (q1 / total)
    l0 = (a0 - mixed) / total * q0 * (1.0 - q0)
    l1 = (a1 - mixed) / total * q1 * (1.0 - q1)
    lane = lax.broadcasted_iota(jnp.int32, (rows, 128), 1).astype(F32)
    cols[...] = jnp.where(lane == r0, l0, 0.0) + jnp.where(lane == r1, l1, 0.0)
    sums_to_core(0, 1).wait_recv()

    def finish_backward(q, _):
        sums_to_link(0, q).wait_recv()
        for k in range(CHUNK // STEP):
            at_rows = pl.ds(pl.multiple_of(q * CHUNK + k * STEP, STEP), STEP)
            far = pl.ds(pl.multiple_of(2 * rows + q * CHUNK + k * STEP, STEP), STEP)
            near = pl.ds(pl.multiple_of(rows + q * CHUNK + k * STEP, STEP), STEP)
            wide = sx[far, :].astype(F32)
            inv = lax.rsqrt(jnp.mean(wide * wide, axis=1, keepdims=True) + EPSILON)
            dn = wb[far, :].astype(F32) + rcb[near, :].astype(F32) + lpb[at_rows, :].astype(F32)
            lcol = cols[at_rows, :]
            for j in range(4):
                dn = dn + lcol[:, j : j + 1] * rout[j : j + 1, :].astype(F32)
            scaled = dn * gain[...]
            mean = jnp.mean(scaled * wide, axis=1, keepdims=True)
            grad = z[far, :].astype(F32) + (inv * scaled - wide * (inv * inv * inv * mean))
            wb[far, :] = grad.astype(BF16)

        @pl.when(c > 0)
        def _():
            result(0, q).start()

        return 0

    early = n_chunks - tiles - 2
    lax.fori_loop(0, early, finish_backward, 0)
    pass_to_core(2).wait_recv()
    forward(1, lambda j: finish_backward(early + j, 0))
    sums_to_core(1, 1).start()
    lax.fori_loop(early + tiles, n_chunks, finish_backward, 0)
    nrm[0:rows, :] = jnp.zeros((rows, width), BF16)

    @pl.when(c == 0)
    def _():
        pltpu.make_async_copy(nrm.at[0:rows], fo_hbm, zero_sem.at[0]).start()

    @pl.when(c == n_pipe - 1)
    def _():
        pltpu.make_async_copy(nrm.at[0:rows], go_hbm, zero_sem.at[1]).start()

    sums_to_core(1, 1).wait_recv()

    def finish_forward(q, _):
        sums_to_link(1, q).wait_recv()
        far = tail(1, q)
        near = pl.ds(pl.multiple_of(rows + q * FINE, FINE), FINE)
        out = wf[far, :].astype(F32) + rcf[near, :].astype(F32) + lpf[part(1, q), :].astype(F32)
        wf[far, :] = (fx[far, :].astype(F32) + out).astype(BF16)

        @pl.when(c < n_pipe - 1)
        def _():
            result(1, q).start()

        return 0

    lax.fori_loop(0, counts[1], finish_forward, 0)

    for s in (1, 2, 3):
        routes_to(s, 0).wait_send()
        routes_to(s, 1).wait_send()
        dots_to(s).wait_send()
    for i in range(3):
        own_to_core(i).wait_send()
        own_to_link(i).wait_send()
        pass_to_core(i).wait_send()
    for i in range(2):
        for g in range(2):
            sums_to_core(i, g).wait_send()
        for q in range(counts[i]):
            sums_to_link(i, q).wait_send()

    @pl.when(c > 0)
    def _():
        for q in range(counts[0]):
            result(0, q).wait_send()
        for q in range(counts[1]):
            result(1, q).wait_recv()

    @pl.when(c < n_pipe - 1)
    def _():
        for q in range(counts[1]):
            result(1, q).wait_send()
        for q in range(counts[0]):
            result(0, q).wait_recv()

    @pl.when(c == 0)
    def _():
        pltpu.make_async_copy(nrm.at[0:rows], fo_hbm, zero_sem.at[0]).wait()

    @pl.when(c == n_pipe - 1)
    def _():
        pltpu.make_async_copy(nrm.at[0:rows], go_hbm, zero_sem.at[1]).wait()


def local(
    n_pipe, fwd_in, fwd_routes, saved_in, saved_routes, grad_in, norm_gain, router, w_gate, w_up, w_down
):
    rows, width = fwd_in.shape
    hidden = w_gate.shape[3]
    tn = min(256, hidden)
    td = 512 if width % 512 == 0 else 128
    n_chunks = rows // CHUNK
    dma = pltpu.SemaphoreType.DMA
    vmem = pl.BlockSpec(memory_space=pltpu.VMEM)
    hbm = pl.BlockSpec(memory_space=pl.ANY)
    grad_out_type = jax.ShapeDtypeStruct((rows, width), BF16)
    held_type = pltpu.VMEM((rows, width), BF16)
    fwd_out, grad_out = pl.pallas_call(
        functools.partial(kernel, n_pipe, tn, td),
        out_shape=(held_type, held_type),
        in_specs=[hbm, hbm, hbm, vmem, vmem, vmem, vmem, hbm, hbm, hbm],
        out_specs=(vmem, vmem),
        scratch_shapes=[
            pltpu.VMEM((4 * rows, width), BF16),
            pltpu.VMEM((4 * rows, width), BF16),
            pltpu.VMEM((4 * rows, width), BF16),
            pltpu.VMEM((2, 4, 2, rows), jnp.int32),
            pltpu.VMEM((width, hidden), BF16),
            pltpu.VMEM((width, hidden), BF16),
            pltpu.VMEM((hidden, width), BF16),
            pltpu.VMEM((128, width), BF16),
            pltpu.VMEM((2 * rows, width), BF16),
            pltpu.VMEM((2 * rows, hidden), BF16),
            pltpu.VMEM((2 * rows, hidden), BF16),
            pltpu.VMEM((2 * rows, hidden), BF16),
            pltpu.VMEM((2 * rows, 128), F32),
            pltpu.VMEM((rows, 128), F32),
            pltpu.VMEM((4 * rows, width), BF16),
            pltpu.VMEM((4 * rows, width), BF16),
            pltpu.VMEM((2 * rows, width), BF16),
            pltpu.VMEM((2 * rows, width), BF16),
            pltpu.VMEM((rows, width), BF16),
            pltpu.VMEM((rows, width), BF16),
            pltpu.VMEM((4, 8, rows), F32),
            pltpu.VMEM((4, 8, rows), F32),
            dma((3,)), dma((3, hidden // tn)),
            dma((10,)), dma((10,)),
            dma((3,)), dma((3,)),
            dma((6,)), dma((6,)),
            dma((3,)), dma((3,)),
            dma((n_chunks,)), dma((n_chunks,)),
            dma((rows // FINE,)), dma((rows // FINE,)),
            dma((n_chunks,)), dma((n_chunks,)),
            dma((rows // FINE,)), dma((rows // FINE,)),
            dma((2,)),
        ],
        compiler_params=pltpu.CompilerParams(
            collective_id=0, has_side_effects=True, vmem_limit_bytes=60 * 1024 * 1024
        ),
        name="relay_slot",
    )(saved_in, grad_in, fwd_in, saved_routes.T, fwd_routes.T, norm_gain, router[0].T, w_gate, w_up, w_down)
    return fwd_out, grad_out


def solution(mesh):
    rows = P(("pipe", "expert"), None)
    in_specs = (
        rows, rows, rows, rows, rows,
        P("pipe", None),
        P("pipe", None, None),
        P("pipe", "expert", None, None),
        P("pipe", "expert", None, None),
        P("pipe", "expert", None, None),
    )
    return jax.shard_map(
        functools.partial(local, mesh.shape["pipe"]),
        mesh=mesh, in_specs=in_specs, out_specs=(rows, rows), check_vma=False,
    )
```
